512 devices in a mesh: wide: 64 (over x, y, core), chain: 8 (over z).
Axes of the slice: x: 4, y: 8, z: 8, core: 2. Of those that a mesh axis runs over, the one named last changes fastest.
Arguments:
- queries: bfloat16 [131072, 1024], P(('chain', 'wide')), may hold values from -4 to 4
- keys: bfloat16 [131072, 1024], P(('chain', 'wide')), may hold values from -4 to 4
- values: bfloat16 [131072, 1024], P(('chain', 'wide')), may hold values from -6 to 6
Outputs:
- attended: bfloat16 [131072, 1024], P(('chain', 'wide'))
The draws below stay inside these ranges and needn't reach their ends.
All inputs are finite; a program needn't handle non-finite values.
Results may differ from the reference program's by a relative error of at most 0.005.
Values may be sent and summed in bfloat16 or wider, within the bound.
A program may use at most 64 MiB of HBM per device.

```python
import jax
import jax.numpy as jnp
from jax import lax

HEADS = 16
HEAD_DIM = 64
TOK_DEV = 256
TOKENS = 131072


def level_of(rng, shape, cuts, least, high):
    def one(position, parts):
        steps = jax.random.uniform(jax.random.fold_in(jax.random.fold_in(rng, 6), position), (parts,), jnp.float32, least / len(cuts), high / len(cuts))
        return jnp.repeat(jnp.exp(steps), shape[position] // parts).reshape((-1,) + (1,) * (len(shape) - position - 1))

    gain = one(*cuts[0])
    for cut in cuts[1:]:
        gain = gain * one(*cut)
    return gain


def scatter_about(rng, extent, width, limit, pieces=(), dtype=jnp.bfloat16):
    level = level_of(rng, extent, pieces, -0.22, 0.18) if pieces else 1.0
    drawn = jax.random.normal(rng, extent, jnp.float32) * width * level
    return jnp.minimum(jnp.maximum(drawn, -limit), limit).astype(dtype)


def setup_inputs(seed: int = 0) -> dict:
    splits = jax.random.split(jax.random.key(seed), 4)
    queries = scatter_about(splits[0], (TOKENS, HEADS * HEAD_DIM), 0.3, 4.0, ((0, 512),))
    keys = scatter_about(splits[1], (TOKENS, HEADS * HEAD_DIM), 0.3, 4.0, ((0, 512),))
    values = scatter_about(splits[2], (TOKENS, HEADS * HEAD_DIM), 1.0, 6.0, ((0, 512),))
    return {"queries": queries, "keys": keys, "values": values}


def reference(queries, keys, values):
    blocks = TOKENS // TOK_DEV
    q_all = queries.reshape(blocks, TOK_DEV, HEADS, HEAD_DIM)
    k_all = keys.reshape(blocks, TOK_DEV, HEADS, HEAD_DIM)
    v_all = values.reshape(blocks, TOK_DEV, HEADS, HEAD_DIM)
    causal = jnp.arange(TOK_DEV)[:, None] >= jnp.arange(TOK_DEV)[None, :]

    def advance(carry, block):
        q_blk, k_blk, v_blk = block
        q32 = q_blk.astype(jnp.float32)
        k32 = k_blk.astype(jnp.float32)
        v32 = v_blk.astype(jnp.float32)
        prefix = carry.astype(jnp.bfloat16).astype(jnp.float32)
        inter = jnp.einsum('the,hef->thf', q32, prefix)
        scores = jnp.einsum('the,she->hts', q32, k32)
        scores = jnp.where(causal[None], scores, 0.0).astype(jnp.bfloat16).astype(jnp.float32)
        intra = jnp.einsum('hts,shf->thf', scores, v32)
        total = intra + inter
        normed = total / jnp.sqrt(lax.optimization_barrier(jnp.mean(total * total, axis=-1, keepdims=True)) + 1e-06)
        state = jnp.einsum('the,thf->hef', k32, v32)
        return (carry + state, normed.astype(jnp.bfloat16))
    start = jnp.zeros((HEADS, HEAD_DIM, HEAD_DIM), jnp.float32)
    final_state, outputs = lax.scan(advance, start, (q_all, k_all, v_all))
    return outputs.reshape(TOKENS, HEADS * HEAD_DIM)
```

```python
import functools

import jax
import jax.numpy as jnp
from jax import lax
from jax.experimental import pallas as pl
from jax.experimental.pallas import tpu as pltpu
from jax.sharding import PartitionSpec as P

HEAD_DIM = 64
PAIR = 2 * HEAD_DIM
PAIRS = 8
LINE = 16
CHIPS = 8
ROWS = 32
BF16 = jnp.bfloat16
F32 = jnp.float32
MESH = pl.DeviceIdType.MESH


def dot(a, b, contract):
    return lax.dot_general(a, b, (contract, ((), ())), preferred_element_type=F32)


def attend_kernel(
    nx, nz, q_hbm, k_hbm, v_hbm, o_ref,
    q, k, v, intra, s_out, s_in, t_out, t_in, z_out, z_in, p_out, p_in,
    in_sem, s_send, s_recv, t_send, t_recv, z_send, z_recv, p_send, p_recv,
):
    tokens = q.shape[0]
    half = tokens // 2
    wide = lax.axis_index("wide")
    z = lax.axis_index("chain")
    x = wide // LINE
    a = lax.rem(wide, LINE)
    y = a // 2
    core = lax.rem(a, 2)
    base = x * LINE

    loads = []
    for i, (src, dst) in enumerate(((k_hbm, k), (v_hbm, v), (q_hbm, q))):
        load = pltpu.make_async_copy(src, dst, in_sem.at[i])
        load.start()
        loads.append(load)

    barrier = pltpu.get_barrier_semaphore()
    for i in range(1, LINE):
        pl.semaphore_signal(
            barrier, inc=1, device_id={"wide": base + lax.rem(a + i, LINE)}, device_id_type=MESH
        )
    for i in range(1, nx):
        pl.semaphore_signal(
            barrier, inc=1, device_id={"wide": lax.rem(x + i, nx) * LINE + a}, device_id_type=MESH
        )
    for i in range(1, nz):
        pl.semaphore_signal(
            barrier, inc=1, device_id={"chain": lax.rem(z + i, nz)}, device_id_type=MESH
        )

    low = lax.broadcasted_iota(jnp.int32, (HEAD_DIM, PAIR), 1) < HEAD_DIM

    def pair_state(p):
        cols = pl.ds(pl.multiple_of(p * PAIR, PAIR), PAIR)
        both = dot(k[:, cols], v[:, cols], ((0,), (0,)))
        packed = jnp.where(low, both[:HEAD_DIM], both[HEAD_DIM:])
        return packed.astype(BF16).reshape(2, ROWS, PAIR)

    def send_piece(dest):
        pltpu.make_async_remote_copy(
            src_ref=s_out.at[dest], dst_ref=s_in.at[a], send_sem=s_send, recv_sem=s_recv,
            device_id={"wide": base + dest}, device_id_type=MESH,
        ).start()

    loads[0].wait()
    loads[1].wait()
    first = True
    for s in (4, 3, 5, 2, 6, 1, 7):
        p = lax.rem(y + s, CHIPS)
        s_out[pl.ds(2 * p, 2)] = pair_state(p)
        if first:
            pl.semaphore_wait(barrier, LINE - 1 + nx - 1 + nz - 1)
            first = False
        send_piece(2 * p)
        send_piece(2 * p + 1)
    s_out[pl.ds(2 * y, 2)] = pair_state(y)
    send_piece(2 * y + 1 - core)
    s_in[a] = s_out[a]

    loads[2].wait()

    upper = lax.broadcasted_iota(jnp.int32, (half, half), 0) >= lax.broadcasted_iota(
        jnp.int32, (half, half), 1
    )
    lower = lax.broadcasted_iota(jnp.int32, (half, tokens), 0) + half >= lax.broadcasted_iota(
        jnp.int32, (half, tokens), 1
    )
    lanes = lax.broadcasted_iota(jnp.int32, (1, PAIR), 1)
    keep = [
        jnp.where(lanes < HEAD_DIM, 1.0, 0.0).astype(BF16),
        jnp.where(lanes >= HEAD_DIM, 1.0, 0.0).astype(BF16),
    ]

    def intra_pair(p):
        cols = slice(p * PAIR, (p + 1) * PAIR)
        top = bottom = 0.0
        for h in range(2):
            kh = k[:, cols] * keep[h]
            vh = v[:, cols] * keep[h]
            s_top = dot(q[:half, cols], kh[:half], ((1,), (1,)))
            s_top = jnp.where(upper, s_top, 0.0).astype(BF16)
            s_bot = dot(q[half:, cols], kh, ((1,), (1,)))
            s_bot = jnp.where(lower, s_bot, 0.0).astype(BF16)
            top = top + dot(s_top, vh[:half], ((1,), (0,)))
            bottom = bottom + dot(s_bot, vh, ((1,), (0,)))
        intra[:half, cols] = top
        intra[half:, cols] = bottom

    for p in range(4):
        intra_pair(p)

    pltpu.make_async_copy(s_in.at[: LINE - 1], s_in.at[: LINE - 1], s_recv).wait()
    total = s_in[0].astype(F32)
    for i in range(1, LINE):
        total = total + s_in[i].astype(F32)
    t_out[...] = total
    for i in range(1, nx):
        pltpu.make_async_remote_copy(
            src_ref=t_out, dst_ref=t_in.at[x], send_sem=t_send.at[i], recv_sem=t_recv,
            device_id={"wide": lax.rem(x + i, nx) * LINE + a}, device_id_type=MESH,
        ).start()
    t_in[x] = total

    for p in range(4, 6):
        intra_pair(p)

    pltpu.make_async_copy(t_in.at[: nx - 1], t_in.at[: nx - 1], t_recv).wait()
    plane = jnp.zeros((ROWS, PAIR), F32)
    before = jnp.zeros((ROWS, PAIR), F32)
    for i in range(nx):
        plane = plane + t_in[i]
        before = before + jnp.where(i < x, t_in[i], 0.0)
    z_out[...] = plane

    def z_copy(other):
        return pltpu.make_async_remote_copy(
            src_ref=z_out, dst_ref=z_in.at[z], send_sem=z_send.at[other], recv_sem=z_recv.at[z],
            device_id={"chain": other}, device_id_type=MESH,
        )

    def z_start(i, _):
        z_copy(z + i).start()
        return 0

    lax.fori_loop(1, nz - z, z_start, 0)

    for p in range(6, 8):
        intra_pair(p)

    def z_take(i, acc):
        pltpu.make_async_copy(z_in.at[i], z_in.at[i], z_recv.at[i]).wait()
        return acc + z_in[i]

    run = lax.fori_loop(0, z, z_take, before)
    for i in range(LINE):
        p_out[i] = run.astype(BF16)
        if i + 1 < LINE:
            run = run + s_in[i].astype(F32)
    p_in[a] = p_out[a]
    for i in (8, 9, 7, 10, 6, 11, 5, 12, 4, 13, 3, 14, 2, 15, 1):
        dest = lax.rem(a + i, LINE)
        pltpu.make_async_remote_copy(
            src_ref=p_out.at[dest], dst_ref=p_in.at[a], send_sem=p_send, recv_sem=p_recv,
            device_id={"wide": base + dest}, device_id_type=MESH,
        ).start()

    mean = jnp.where(
        (lax.broadcasted_iota(jnp.int32, (PAIR, PAIR), 0) < HEAD_DIM)
        == (lax.broadcasted_iota(jnp.int32, (PAIR, PAIR), 1) < HEAD_DIM),
        1.0 / HEAD_DIM, 0.0,
    ).astype(BF16)
    pltpu.make_async_copy(p_in.at[: LINE - 1], p_in.at[: LINE - 1], p_recv).wait()
    for p in range(PAIRS):
        cols = slice(p * PAIR, (p + 1) * PAIR)
        prefix = p_in[2 * p : 2 * p + 2].reshape(HEAD_DIM, PAIR)
        prefix = jnp.concatenate([prefix * keep[0], prefix * keep[1]], axis=0)
        value = intra[:, cols] + dot(q[:, cols], prefix, ((1,), (0,)))
        square = value * value
        coarse = square.astype(BF16)
        fine = (square - coarse.astype(F32)).astype(BF16)
        var = dot(coarse, mean, ((1,), (0,))) + dot(fine, mean, ((1,), (0,)))
        o_ref[:, cols] = (value * lax.rsqrt(var + 1e-06)).astype(BF16)

    pltpu.make_async_copy(s_out.at[: LINE - 1], s_out.at[: LINE - 1], s_send).wait()
    for i in range(1, nx):
        pltpu.make_async_copy(t_out, t_out, t_send.at[i]).wait()

    def z_done(i, _):
        pltpu.make_async_copy(z_out, z_out, z_send.at[z + i]).wait()
        return 0

    lax.fori_loop(1, nz - z, z_done, 0)
    pltpu.make_async_copy(p_out.at[: LINE - 1], p_out.at[: LINE - 1], p_send).wait()


def solution(mesh):
    nx = mesh.shape["wide"] // LINE
    nz = mesh.shape["chain"]

    def per_device(queries, keys, values):
        tokens, width = queries.shape
        dma = pltpu.SemaphoreType.DMA
        return pl.pallas_call(
            functools.partial(attend_kernel, nx, nz),
            out_shape=jax.ShapeDtypeStruct((tokens, width), BF16),
            in_specs=[pl.BlockSpec(memory_space=pltpu.HBM)] * 3,
            out_specs=pl.BlockSpec(memory_space=pltpu.VMEM),
            scratch_shapes=[
                pltpu.VMEM((tokens, width), BF16),
                pltpu.VMEM((tokens, width), BF16),
                pltpu.VMEM((tokens, width), BF16),
                pltpu.VMEM((tokens, width), F32),
                pltpu.VMEM((LINE, ROWS, PAIR), BF16),
                pltpu.VMEM((LINE, ROWS, PAIR), BF16),
                pltpu.VMEM((ROWS, PAIR), F32),
                pltpu.VMEM((nx, ROWS, PAIR), F32),
                pltpu.VMEM((ROWS, PAIR), F32),
                pltpu.VMEM((nz, ROWS, PAIR), F32),
                pltpu.VMEM((LINE, ROWS, PAIR), BF16),
                pltpu.VMEM((LINE, ROWS, PAIR), BF16),
                dma((3,)),
                dma,
                dma,
                dma((nx,)),
                dma,
                dma((nz,)),
                dma((nz,)),
                dma,
                dma,
            ],
            compiler_params=pltpu.CompilerParams(
                collective_id=0, has_side_effects=True, vmem_limit_bytes=32 << 20
            ),
        )(*(pltpu.with_memory_space_constraint(t, pltpu.HBM) for t in (queries, keys, values)))

    placed = P(("chain", "wide"), None)
    return jax.shard_map(
        per_device, mesh=mesh, in_specs=(placed,) * 3, out_specs=placed, check_vma=False
    )
```

```python
import functools

import jax
import jax.numpy as jnp
from jax import lax
from jax.experimental import pallas as pl
from jax.experimental.pallas import tpu as pltpu
from jax.sharding import PartitionSpec as P

HEAD_DIM = 64
PAIR = 2 * HEAD_DIM
PAIRS = 8
HALF = PAIRS // 2
CHIPS = 8
ROWS = 8
STATE = HALF * HEAD_DIM
QUAD = 2 * PAIR
BF16 = jnp.bfloat16
F32 = jnp.float32
MESH = pl.DeviceIdType.MESH


def dot(a, b, contract):
    return lax.dot_general(a, b, (contract, ((), ())), preferred_element_type=F32)


def attend_kernel(
    nx, nz, q_hbm, k_hbm, v_hbm, o_ref,
    q, k, v, intra, given, mine, theirs, first, s_out, s_in, z_out, z_in, p_out, p_in, p_other,
    in_sem, mate_send, mate_recv, s_send, s_recv, z_send, z_recv, p_send, p_recv, f_send, f_recv,
    mate_here, all_here, z_ready,
):
    tokens = q.shape[0]
    row_half = tokens // 2
    members = nx * CHIPS
    wide = lax.axis_index("wide")
    z = lax.axis_index("chain")
    chip = wide // 2
    core = lax.rem(wide, 2)
    mate = {"wide": 2 * chip + 1 - core}
    mid = nz // 2
    z_from = jnp.where(z < mid, 0, mid - 1)
    z_to = jnp.where(z < mid - 1, mid, nz)
    x, y = chip // CHIPS, lax.rem(chip, CHIPS)
    away = [(i, j) for i in range(nx) for j in range(CHIPS) if i or j]
    away.sort(key=lambda d: -min(d[0], nx - d[0]) - min(d[1], CHIPS - d[1]))
    peers = [lax.rem(x + i, nx) * CHIPS + lax.rem(y + j, CHIPS) for i, j in away]

    def plane_id(chip):
        return {"wide": 2 * chip + core}

    def z_id(i):
        return {"chain": i}

    loads = []
    for c in range(4):
        half = 1 - core if c < 2 else core
        cols = pl.ds(pl.multiple_of(half * (HALF * PAIR) + (c % 2) * QUAD, QUAD), QUAD)
        pair = [
            pltpu.make_async_copy(k_hbm.at[:, cols], k.at[:, cols], in_sem.at[2 * c]),
            pltpu.make_async_copy(v_hbm.at[:, cols], v.at[:, cols], in_sem.at[2 * c + 1]),
        ]
        for load in pair:
            load.start()
        loads.append(pair)
    q_load = pltpu.make_async_copy(q_hbm, q, in_sem.at[8])
    q_load.start()

    barrier = pltpu.get_barrier_semaphore()

    @pl.when(core == 1)
    def _():
        pl.semaphore_signal(barrier, inc=1, device_id=mate, device_id_type=MESH)

    @pl.when(core == 0)
    def _():
        pl.semaphore_wait(barrier, 1)
        pl.semaphore_signal(mate_here, inc=1, device_id=mate, device_id_type=MESH)

    @pl.when(core == 1)
    def _():
        pl.semaphore_wait(mate_here, 1)
        for chip_there in peers:
            pl.semaphore_signal(
                barrier, inc=1, device_id=plane_id(chip_there), device_id_type=MESH
            )

        def greet(i, _):
            pl.semaphore_signal(barrier, inc=1, device_id=z_id(i), device_id_type=MESH)
            return 0

        lax.fori_loop(z + 1, z_to, greet, 0)

    low = lax.broadcasted_iota(jnp.int32, (HEAD_DIM, PAIR), 1) < HEAD_DIM

    def pair_state(half, j):
        cols = pl.ds(pl.multiple_of((half * HALF + j) * PAIR, PAIR), PAIR)
        both = dot(k[:, cols], v[:, cols], ((0,), (0,)))
        return jnp.where(low, both[:HEAD_DIM], both[HEAD_DIM:])

    def half_state(half, first_load, out):
        for j in range(HALF):
            if j % 2 == 0:
                for load in loads[first_load + j // 2]:
                    load.wait()
            out[j * HEAD_DIM : (j + 1) * HEAD_DIM] = pair_state(half, j)

    half_state(1 - core, 0, given)

    swap = pltpu.make_async_remote_copy(
        src_ref=given, dst_ref=theirs, send_sem=mate_send.at[0],
        recv_sem=mate_recv.at[0], device_id=mate, device_id_type=MESH,
    )
    swap.start()
    half_state(core, 2, mine)
    extra = pltpu.make_async_remote_copy(
        src_ref=mine, dst_ref=first, send_sem=mate_send.at[1], recv_sem=mate_recv.at[1],
        device_id=mate, device_id_type=MESH,
    )

    @pl.when(core == 0)
    def _():
        extra.start()

    swap.wait_recv()
    for i in range(members):
        rows = slice(i * ROWS, (i + 1) * ROWS)
        s_out[i] = (mine[rows] + theirs[rows]).astype(BF16)

    @pl.when(core == 1)
    def _():
        pl.semaphore_wait(barrier, members - 1 + z - z_from)
        pl.semaphore_signal(all_here, inc=1, device_id=mate, device_id_type=MESH)

    @pl.when(core == 0)
    def _():
        pl.semaphore_wait(all_here, 1)

    for chip_there in peers:
        pltpu.make_async_remote_copy(
            src_ref=s_out.at[chip_there], dst_ref=s_in.at[chip], send_sem=s_send, recv_sem=s_recv,
            device_id=plane_id(chip_there), device_id_type=MESH,
        ).start()

    s_in[chip] = s_out[chip]

    def answer_z(i, _):
        pl.semaphore_signal(z_ready.at[z], inc=1, device_id=z_id(i), device_id_type=MESH)
        return 0

    lax.fori_loop(z_from, z, answer_z, 0)

    upper = lax.broadcasted_iota(jnp.int32, (row_half, row_half), 0) >= lax.broadcasted_iota(
        jnp.int32, (row_half, row_half), 1
    )
    lower = lax.broadcasted_iota(
        jnp.int32, (row_half, tokens), 0
    ) + row_half >= lax.broadcasted_iota(jnp.int32, (row_half, tokens), 1)
    lanes = lax.broadcasted_iota(jnp.int32, (1, PAIR), 1)
    keep = [
        jnp.where(lanes < HEAD_DIM, 1.0, 0.0).astype(BF16),
        jnp.where(lanes >= HEAD_DIM, 1.0, 0.0).astype(BF16),
    ]

    def spread(packed):
        return jnp.concatenate([packed * keep[0], packed * keep[1]], axis=0)

    def intra_pair(p, _):
        cols = pl.ds(pl.multiple_of(p * PAIR, PAIR), PAIR)
        qp, kp, vp = q[:, cols], k[:, cols], v[:, cols]
        top = bottom = 0.0
        for h in range(2):
            kh = kp * keep[h]
            vh = vp * keep[h]
            s_top = dot(qp[:row_half], kh[:row_half], ((1,), (1,)))
            s_top = jnp.where(upper, s_top, 0.0).astype(BF16)
            s_bot = dot(qp[row_half:], kh, ((1,), (1,)))
            s_bot = jnp.where(lower, s_bot, 0.0).astype(BF16)
            top = top + dot(s_top, vh[:row_half], ((1,), (0,)))
            bottom = bottom + dot(s_bot, vh, ((1,), (0,)))
        intra[:row_half, cols] = top
        intra[row_half:, cols] = bottom
        return 0

    q_load.wait()
    lax.fori_loop(0, PAIRS, intra_pair, 0)

    @pl.when(core == 1)
    def _():
        extra.wait_recv()
        for p in range(PAIRS):
            cols = slice(p * PAIR, (p + 1) * PAIR)
            rows = slice((p % HALF) * HEAD_DIM, (p % HALF + 1) * HEAD_DIM)
            state = (first if p < HALF else theirs)[rows].astype(BF16)
            intra[:, cols] += dot(q[:, cols], spread(state), ((1,), (0,)))

    @pl.when(core == 0)
    def _():
        extra.wait_send()

    pltpu.make_async_copy(s_in.at[: members - 1], s_in.at[: members - 1], s_recv).wait()
    plane = s_in[0].astype(F32)
    for i in range(1, members):
        plane = plane + s_in[i].astype(F32)

    def z_start(i, _):
        pl.semaphore_wait(z_ready.at[i], 1)
        pltpu.make_async_remote_copy(
            src_ref=z_out, dst_ref=z_in.at[z], send_sem=z_send.at[i], recv_sem=z_recv.at[z],
            device_id=z_id(i), device_id_type=MESH,
        ).start()
        return 0

    def z_take(i, acc):
        pltpu.make_async_copy(z_in.at[i], z_in.at[i], z_recv.at[i]).wait()
        return acc + z_in[i]

    @pl.when(z != mid - 1)
    def _():
        z_out[...] = plane
        lax.fori_loop(z + 1, z_to, z_start, 0)

    run = lax.fori_loop(z_from, z, z_take, jnp.zeros((ROWS, PAIR), F32))

    @pl.when(z == mid - 1)
    def _():
        z_out[...] = run + plane
        lax.fori_loop(z + 1, z_to, z_start, 0)

    for i in range(members):
        p_out[i] = run.astype(BF16)
        if i + 1 < members:
            run = run + s_in[i].astype(F32)

    for chip_there in peers:
        pltpu.make_async_remote_copy(
            src_ref=p_out.at[chip_there], dst_ref=p_in.at[chip], send_sem=p_send, recv_sem=p_recv,
            device_id=plane_id(chip_there), device_id_type=MESH,
        ).start()

    p_in[chip] = p_out[chip]

    swap.wait_send()
    pltpu.make_async_copy(s_out.at[: members - 1], s_out.at[: members - 1], s_send).wait()

    def z_done(i, _):
        pltpu.make_async_copy(z_out, z_out, z_send.at[i]).wait()
        return 0

    lax.fori_loop(z + 1, z_to, z_done, 0)

    mean = jnp.where(
        lax.broadcasted_iota(jnp.int32, (QUAD, QUAD), 0) // HEAD_DIM
        == lax.broadcasted_iota(jnp.int32, (QUAD, QUAD), 1) // HEAD_DIM,
        1.0 / HEAD_DIM, 0.0,
    ).astype(BF16)
    zeros = jnp.zeros((PAIR, PAIR), BF16)

    def finish(half, pieces):
        for j in range(0, HALF, 2):
            cols = pl.ds(pl.multiple_of((half * HALF + j) * PAIR, QUAD), QUAD)
            n = HEAD_DIM // ROWS
            one = spread(pieces[j * n : (j + 1) * n].reshape(HEAD_DIM, PAIR))
            two = spread(pieces[(j + 1) * n : (j + 2) * n].reshape(HEAD_DIM, PAIR))
            prefix = jnp.concatenate(
                [jnp.concatenate([one, zeros], axis=1), jnp.concatenate([zeros, two], axis=1)],
                axis=0,
            )
            value = intra[:, cols] + dot(q[:, cols], prefix, ((1,), (0,)))
            square = value * value
            coarse = square.astype(BF16)
            fine = (square - coarse.astype(F32)).astype(BF16)
            var = dot(coarse, mean, ((1,), (0,))) + dot(fine, mean, ((1,), (0,)))
            o_ref[:, cols] = (value * lax.rsqrt(var + 1e-06)).astype(BF16)

    pltpu.make_async_copy(p_in.at[: members - 1], p_in.at[: members - 1], p_recv).wait()
    forward = pltpu.make_async_remote_copy(
        src_ref=p_in, dst_ref=p_other, send_sem=f_send, recv_sem=f_recv,
        device_id=mate, device_id_type=MESH,
    )
    forward.start()
    finish(core, p_in)
    forward.wait_recv()
    finish(1 - core, p_other)
    forward.wait_send()
    pltpu.make_async_copy(p_out.at[: members - 1], p_out.at[: members - 1], p_send).wait()


def solution(mesh):
    nx = mesh.shape["wide"] // (2 * CHIPS)
    nz = mesh.shape["chain"]
    members = nx * CHIPS

    def per_device(queries, keys, values):
        tokens, width = queries.shape
        dma = pltpu.SemaphoreType.DMA
        plain = pltpu.SemaphoreType.REGULAR
        in_hbm = [pltpu.with_memory_space_constraint(t, pltpu.HBM) for t in (queries, keys, values)]
        return pl.pallas_call(
            functools.partial(attend_kernel, nx, nz),
            out_shape=jax.ShapeDtypeStruct((tokens, width), BF16),
            in_specs=[pl.BlockSpec(memory_space=pltpu.HBM)] * 3,
            out_specs=pl.BlockSpec(memory_space=pltpu.VMEM),
            scratch_shapes=[
                pltpu.VMEM((tokens, width), BF16),
                pltpu.VMEM((tokens, width), BF16),
                pltpu.VMEM((tokens, width), BF16),
                pltpu.VMEM((tokens, width), F32),
                pltpu.VMEM((STATE, PAIR), F32),
                pltpu.VMEM((STATE, PAIR), F32),
                pltpu.VMEM((STATE, PAIR), F32),
                pltpu.VMEM((STATE, PAIR), F32),
                pltpu.VMEM((members, ROWS, PAIR), BF16),
                pltpu.VMEM((members, ROWS, PAIR), BF16),
                pltpu.VMEM((ROWS, PAIR), F32),
                pltpu.VMEM((nz, ROWS, PAIR), F32),
                pltpu.VMEM((members, ROWS, PAIR), BF16),
                pltpu.VMEM((members, ROWS, PAIR), BF16),
                pltpu.VMEM((members, ROWS, PAIR), BF16),
                dma((9,)),
                dma((2,)),
                dma((2,)),
                dma,
                dma,
                dma((nz,)),
                dma((nz,)),
                dma,
                dma,
                dma,
                dma,
                plain,
                plain,
                plain((nz,)),
            ],
            compiler_params=pltpu.CompilerParams(
                collective_id=0, has_side_effects=True, vmem_limit_bytes=32 << 20
            ),
        )(*in_hbm)

    placed = P(("chain", "wide"), None)
    return jax.shard_map(
        per_device, mesh=mesh, in_specs=(placed,) * 3, out_specs=placed, check_vma=False
    )
```

```python
import functools

import jax
import jax.numpy as jnp
from jax import lax
from jax.experimental import pallas as pl
from jax.experimental.pallas import tpu as pltpu
from jax.sharding import PartitionSpec as P

HEAD_DIM = 64
PAIR = 2 * HEAD_DIM
PAIRS = 8
HALF = PAIRS // 2
CHIPS = 8
OWNED = (0, 1)
GREETED = (5, 4, 6, 3, 7, 2, 1, 0)
ROWS = 64 // len(OWNED)
STATE = HALF * HEAD_DIM
QUAD = 2 * PAIR
BF16 = jnp.bfloat16
F32 = jnp.float32
MESH = pl.DeviceIdType.MESH


def dot(a, b, contract):
    return lax.dot_general(a, b, (contract, ((), ())), preferred_element_type=F32)


def attend_kernel(
    nx, nz, q_hbm, k_hbm, v_hbm, o_ref,
    q, k, v, intra, given, mine, theirs, first, s_out, s_in, z_out, z_in, p_out, p_in, p_other,
    in_sem, mate_send, mate_recv, s_send, s_recv, z_send, z_recv, p_send, p_recv, f_send, f_recv,
    mate_here, all_here, z_ready,
):
    tokens = q.shape[0]
    row_half = tokens // 2
    members = nx * CHIPS
    owners = nx * len(OWNED)
    wide = lax.axis_index("wide")
    z = lax.axis_index("chain")
    chip = wide // 2
    core = lax.rem(wide, 2)
    mate = {"wide": 2 * chip + 1 - core}
    x, y = chip // CHIPS, lax.rem(chip, CHIPS)
    place = sum(jnp.where(y == there, i, 0) for i, there in enumerate(OWNED))
    owns = functools.reduce(jnp.logical_or, [y == there for there in OWNED])
    owner = x * len(OWNED) + place
    near = sorted(range(nx), key=lambda d: min(d, nx - d))
    far = near[::-1]

    def plane_id(chip):
        return {"wide": 2 * chip + core}

    def z_id(i):
        return {"chain": i}

    def to_plane(columns, across, act):
        for there in columns:
            for d in across:
                chip_there = lax.rem(x + d, nx) * CHIPS + there
                if d:
                    act(chip_there)
                else:
                    pl.when(there != y)(functools.partial(act, chip_there))

    def owner_of(chip):
        column = lax.rem(chip, CHIPS)
        place = sum(jnp.where(column == there, i, 0) for i, there in enumerate(OWNED))
        return chip // CHIPS * len(OWNED) + place

    loads = []
    for c in range(4):
        half = 1 - core if c < 2 else core
        cols = pl.ds(pl.multiple_of(half * (HALF * PAIR) + (c % 2) * QUAD, QUAD), QUAD)
        pair = [
            pltpu.make_async_copy(k_hbm.at[:, cols], k.at[:, cols], in_sem.at[2 * c]),
            pltpu.make_async_copy(v_hbm.at[:, cols], v.at[:, cols], in_sem.at[2 * c + 1]),
        ]
        for load in pair:
            load.start()
        loads.append(pair)
    q_load = pltpu.make_async_copy(q_hbm, q, in_sem.at[8])
    q_load.start()

    barrier = pltpu.get_barrier_semaphore()

    @pl.when(core == 1)
    def _():
        pl.semaphore_signal(barrier, inc=1, device_id=mate, device_id_type=MESH)

    def greet(chip_there, plane_there=z):
        pl.semaphore_signal(
            barrier, inc=1, device_id={"wide": 2 * chip_there + 1, "chain": plane_there},
            device_id_type=MESH,
        )

    @pl.when(owns)
    def _():
        to_plane(GREETED, far, greet)

        def greet_later(i, _):
            greet(chip, i)
            return 0

        lax.fori_loop(z + 1, nz, greet_later, 0)

    @pl.when(core == 0)
    def _():
        pl.semaphore_wait(barrier, 1)
        pl.semaphore_signal(mate_here, inc=1, device_id=mate, device_id_type=MESH)

    @pl.when(core == 1)
    def _():
        pl.semaphore_wait(mate_here, 1)

    low = lax.broadcasted_iota(jnp.int32, (HEAD_DIM, PAIR), 1) < HEAD_DIM

    def pair_state(half, j):
        cols = pl.ds(pl.multiple_of((half * HALF + j) * PAIR, PAIR), PAIR)
        both = dot(k[:, cols], v[:, cols], ((0,), (0,)))
        return jnp.where(low, both[:HEAD_DIM], both[HEAD_DIM:])

    def half_state(half, first_load, out):
        for j in range(HALF):
            if j % 2 == 0:
                for load in loads[first_load + j // 2]:
                    load.wait()
            out[j * HEAD_DIM : (j + 1) * HEAD_DIM] = pair_state(half, j)

    half_state(1 - core, 0, given)

    swap = pltpu.make_async_remote_copy(
        src_ref=given, dst_ref=theirs, send_sem=mate_send.at[0],
        recv_sem=mate_recv.at[0], device_id=mate, device_id_type=MESH,
    )
    swap.start()
    half_state(core, 2, mine)
    extra = pltpu.make_async_remote_copy(
        src_ref=mine, dst_ref=first, send_sem=mate_send.at[1], recv_sem=mate_recv.at[1],
        device_id=mate, device_id_type=MESH,
    )

    @pl.when(core == 0)
    def _():
        extra.start()

    swap.wait_recv()
    for i in range(owners):
        rows = slice(i * ROWS, (i + 1) * ROWS)
        s_out[i] = (mine[rows] + theirs[rows]).astype(BF16)

    @pl.when((core == 1) & owns)
    def _():
        pl.semaphore_wait(barrier, 2 * (owners - 1 + z))

    @pl.when((core == 1) & jnp.logical_not(owns))
    def _():
        pl.semaphore_wait(barrier, 2 * owners)

    @pl.when(core == 1)
    def _():
        pl.semaphore_signal(all_here, inc=1, device_id=mate, device_id_type=MESH)

    @pl.when(core == 0)
    def _():
        pl.semaphore_wait(all_here, 1)

    def send_piece(there):
        pltpu.make_async_remote_copy(
            src_ref=s_out.at[owner_of(there)], dst_ref=s_in.at[chip], send_sem=s_send, recv_sem=s_recv,
            device_id=plane_id(there), device_id_type=MESH,
        ).start()

    to_plane(OWNED, far, send_piece)

    @pl.when(owns)
    def _():
        s_in[chip] = s_out[owner]

        def answer_z(i, _):
            pl.semaphore_signal(z_ready.at[z], inc=1, device_id=z_id(i), device_id_type=MESH)
            return 0

        lax.fori_loop(0, z, answer_z, 0)

    upper = lax.broadcasted_iota(jnp.int32, (row_half, row_half), 0) >= lax.broadcasted_iota(
        jnp.int32, (row_half, row_half), 1
    )
    lower = lax.broadcasted_iota(
        jnp.int32, (row_half, tokens), 0
    ) + row_half >= lax.broadcasted_iota(jnp.int32, (row_half, tokens), 1)
    lanes = lax.broadcasted_iota(jnp.int32, (1, PAIR), 1)
    keep = [
        jnp.where(lanes < HEAD_DIM, 1.0, 0.0).astype(BF16),
        jnp.where(lanes >= HEAD_DIM, 1.0, 0.0).astype(BF16),
    ]

    def spread(packed):
        return jnp.concatenate([packed * keep[0], packed * keep[1]], axis=0)

    def intra_pair(p, _):
        cols = pl.ds(pl.multiple_of(p * PAIR, PAIR), PAIR)
        qp, kp, vp = q[:, cols], k[:, cols], v[:, cols]
        top = bottom = 0.0
        for h in range(2):
            kh = kp * keep[h]
            vh = vp * keep[h]
            s_top = dot(qp[:row_half], kh[:row_half], ((1,), (1,)))
            s_top = jnp.where(upper, s_top, 0.0).astype(BF16)
            s_bot = dot(qp[row_half:], kh, ((1,), (1,)))
            s_bot = jnp.where(lower, s_bot, 0.0).astype(BF16)
            top = top + dot(s_top, vh[:row_half], ((1,), (0,)))
            bottom = bottom + dot(s_bot, vh, ((1,), (0,)))
        intra[:row_half, cols] = top
        intra[row_half:, cols] = bottom
        return 0

    q_load.wait()
    lax.fori_loop(0, PAIRS, intra_pair, 0)

    @pl.when(core == 1)
    def _():
        extra.wait_recv()
        for p in range(PAIRS):
            cols = slice(p * PAIR, (p + 1) * PAIR)
            rows = slice((p % HALF) * HEAD_DIM, (p % HALF + 1) * HEAD_DIM)
            state = (first if p < HALF else theirs)[rows].astype(BF16)
            intra[:, cols] += dot(q[:, cols], spread(state), ((1,), (0,)))

    @pl.when(core == 0)
    def _():
        extra.wait_send()

    def z_start(i, _):
        pl.semaphore_wait(z_ready.at[i], 1)
        pltpu.make_async_remote_copy(
            src_ref=z_out, dst_ref=z_in.at[z], send_sem=z_send.at[i], recv_sem=z_recv.at[z],
            device_id=z_id(i), device_id_type=MESH,
        ).start()
        return 0

    def z_take(i, acc):
        pltpu.make_async_copy(z_in.at[i], z_in.at[i], z_recv.at[i]).wait()
        return acc + z_in[i]

    def z_done(i, _):
        pltpu.make_async_copy(z_out, z_out, z_send.at[i]).wait()
        return 0

    def send_back(there):
        pltpu.make_async_remote_copy(
            src_ref=p_out.at[there], dst_ref=p_in.at[owner], send_sem=p_send, recv_sem=p_recv.at[x // 2],
            device_id=plane_id(there), device_id_type=MESH,
        ).start()

    def wait_for(buffer, count, sem):
        pltpu.make_async_copy(buffer.at[:count], buffer.at[:count], sem).wait()

    @pl.when(owns)
    def _():
        wait_for(s_in, members - 1, s_recv)
        plane = s_in[0].astype(F32)
        for i in range(1, members):
            plane = plane + s_in[i].astype(F32)
        z_out[...] = plane
        lax.fori_loop(z + 1, nz, z_start, 0)
        run = lax.fori_loop(0, z, z_take, jnp.zeros((ROWS, PAIR), F32))
        for i in range(members):
            p_out[i] = run.astype(BF16)
            if i + 1 < members:
                run = run + s_in[i].astype(F32)
        to_plane(range(CHIPS), far, send_back)
        p_in[owner] = p_out[chip]
        wait_for(s_out, owners - 1, s_send)
        lax.fori_loop(z + 1, nz, z_done, 0)

    @pl.when(jnp.logical_not(owns))
    def _():
        wait_for(s_out, owners, s_send)

    swap.wait_send()
    mean = jnp.where(
        lax.broadcasted_iota(jnp.int32, (QUAD, QUAD), 0) // HEAD_DIM
        == lax.broadcasted_iota(jnp.int32, (QUAD, QUAD), 1) // HEAD_DIM,
        1.0 / HEAD_DIM, 0.0,
    ).astype(BF16)
    zeros = jnp.zeros((PAIR, PAIR), BF16)

    def finish(half, part, pieces):
        cols = pl.ds(pl.multiple_of((half * HALF + part * 2) * PAIR, QUAD), QUAD)
        both = pieces[pl.ds(part * share, share)].reshape(2 * HEAD_DIM, PAIR)
        one, two = spread(both[:HEAD_DIM]), spread(both[HEAD_DIM:])
        prefix = jnp.concatenate(
            [jnp.concatenate([one, zeros], axis=1), jnp.concatenate([zeros, two], axis=1)], axis=0
        )
        value = intra[:, cols] + dot(q[:, cols], prefix, ((1,), (0,)))
        square = value * value
        coarse = square.astype(BF16)
        fine = (square - coarse.astype(F32)).astype(BF16)
        var = dot(coarse, mean, ((1,), (0,))) + dot(fine, mean, ((1,), (0,)))
        o_ref[:, cols] = (value * lax.rsqrt(var + 1e-06)).astype(BF16)

    parts = [x // 2, 1 - x // 2]
    share = owners // 2

    def forward(part):
        place = pl.ds(part * share, share)
        return pltpu.make_async_remote_copy(
            src_ref=p_in.at[place], dst_ref=p_other.at[place], send_sem=f_send.at[part],
            recv_sem=f_recv.at[part], device_id=mate, device_id_type=MESH,
        )

    for step, part in enumerate(parts):

        def arrive(count):
            wait_for(p_in, count, p_recv.at[part])

        if step == 0:
            pl.when(owns)(functools.partial(arrive, share - 1))
            pl.when(jnp.logical_not(owns))(functools.partial(arrive, share))
        else:
            arrive(share)
        forward(part).start()
        finish(core, part, p_in)
    for part in parts:
        forward(part).wait_recv()
        finish(1 - core, part, p_other)
    for part in parts:
        forward(part).wait_send()

    @pl.when(owns)
    def _():
        wait_for(p_out, members - 1, p_send)


def solution(mesh):
    nx = mesh.shape["wide"] // (2 * CHIPS)
    nz = mesh.shape["chain"]
    members, owners = nx * CHIPS, nx * len(OWNED)

    def per_device(queries, keys, values):
        tokens, width = queries.shape
        dma = pltpu.SemaphoreType.DMA
        plain = pltpu.SemaphoreType.REGULAR
        in_hbm = [pltpu.with_memory_space_constraint(t, pltpu.HBM) for t in (queries, keys, values)]
        return pl.pallas_call(
            functools.partial(attend_kernel, nx, nz),
            out_shape=jax.ShapeDtypeStruct((tokens, width), BF16),
            in_specs=[pl.BlockSpec(memory_space=pltpu.HBM)] * 3,
            out_specs=pl.BlockSpec(memory_space=pltpu.VMEM),
            scratch_shapes=[
                pltpu.VMEM((tokens, width), BF16),
                pltpu.VMEM((tokens, width), BF16),
                pltpu.VMEM((tokens, width), BF16),
                pltpu.VMEM((tokens, width), F32),
                pltpu.VMEM((STATE, PAIR), F32),
                pltpu.VMEM((STATE, PAIR), F32),
                pltpu.VMEM((STATE, PAIR), F32),
                pltpu.VMEM((STATE, PAIR), F32),
                pltpu.VMEM((owners, ROWS, PAIR), BF16),
                pltpu.VMEM((members, ROWS, PAIR), BF16),
                pltpu.VMEM((ROWS, PAIR), F32),
                pltpu.VMEM((nz, ROWS, PAIR), F32),
                pltpu.VMEM((members, ROWS, PAIR), BF16),
                pltpu.VMEM((owners, ROWS, PAIR), BF16),
                pltpu.VMEM((owners, ROWS, PAIR), BF16),
                dma((9,)),
                dma((2,)),
                dma((2,)),
                dma,
                dma,
                dma((nz,)),
                dma((nz,)),
                dma,
                dma((2,)),
                dma((2,)),
                dma((2,)),
                plain,
                plain,
                plain((nz,)),
            ],
            compiler_params=pltpu.CompilerParams(
                collective_id=0, has_side_effects=True, vmem_limit_bytes=32 << 20
            ),
        )(*in_hbm)

    placed = P(("chain", "wide"), None)
    return jax.shard_map(
        per_device, mesh=mesh, in_specs=(placed,) * 3, out_specs=placed, check_vma=False
    )
```

```python
import functools

import jax
import jax.numpy as jnp
from jax import lax
from jax.experimental import pallas as pl
from jax.experimental.pallas import tpu as pltpu
from jax.sharding import PartitionSpec as P

HEAD_DIM = 64
PAIR = 2 * HEAD_DIM
PAIRS = 8
HALF = PAIRS // 2
CHIPS = 8
OWNED = 2
GREETED = (5, 4, 6, 3, 7, 2, 1, 0)
ROWS = 64 // OWNED
STATE = HALF * HEAD_DIM
QUAD = 2 * PAIR
BF16 = jnp.bfloat16
F32 = jnp.float32
MESH = pl.DeviceIdType.MESH


def dot(a, b, contract):
    return lax.dot_general(a, b, (contract, ((), ())), preferred_element_type=F32)


def attend_kernel(
    nx, nz, q_hbm, k_hbm, v_hbm, o_ref,
    q, k, v, intra, given, mine, theirs, first, s_out, s_in, z_out, z_in, p_out, p_in, p_other,
    in_sem, mate_send, mate_recv, s_send, s_recv, z_send, z_recv, p_send, p_recv, f_send, f_recv,
    mate_here, all_here, z_ready,
):
    tokens = q.shape[0]
    row_half = tokens // 2
    members = nx * CHIPS
    owners = nx * OWNED
    wide = lax.axis_index("wide")
    z = lax.axis_index("chain")
    chip = wide // 2
    core = lax.rem(wide, 2)
    mate = {"wide": 2 * chip + 1 - core}
    x, y = chip // CHIPS, lax.rem(chip, CHIPS)
    def shift(x_there, z_there):
        return jnp.where((x_there == 0) & (z_there == 0), 1, 0)

    offset = shift(x, z)
    owns = (y >= offset) & (y < offset + OWNED)
    owner = x * OWNED + y - offset
    far = sorted(range(nx), key=lambda d: -min(d, nx - d))

    def plane_id(chip):
        return {"wide": 2 * chip + core}

    def z_chip(i):
        return chip - offset + shift(x, i)

    def z_id(i):
        return {"wide": 2 * z_chip(i) + core, "chain": i}

    def to_plane(columns, across, act):
        for there in columns:
            for d in across:
                chip_there = lax.rem(x + d, nx) * CHIPS + there
                if d:
                    act(chip_there)
                else:
                    pl.when(there != y)(functools.partial(act, chip_there))

    def to_owners(act):
        for i in range(OWNED):
            for d in far:
                x_there = lax.rem(x + d, nx)
                chip_there = x_there * CHIPS + i + shift(x_there, z)
                pl.when(chip_there != chip)(
                    functools.partial(act, chip_there, x_there * OWNED + i)
                )

    loads = []
    for c in range(4):
        half = 1 - core if c < 2 else core
        cols = pl.ds(pl.multiple_of(half * (HALF * PAIR) + (c % 2) * QUAD, QUAD), QUAD)
        pair = [
            pltpu.make_async_copy(k_hbm.at[:, cols], k.at[:, cols], in_sem.at[2 * c]),
            pltpu.make_async_copy(v_hbm.at[:, cols], v.at[:, cols], in_sem.at[2 * c + 1]),
        ]
        for load in pair:
            load.start()
        loads.append(pair)
    q_load = pltpu.make_async_copy(q_hbm, q, in_sem.at[8])
    q_load.start()

    barrier = pltpu.get_barrier_semaphore()

    @pl.when(core == 1)
    def _():
        pl.semaphore_signal(barrier, inc=1, device_id=mate, device_id_type=MESH)

    def greet(chip_there, plane_there=z):
        pl.semaphore_signal(
            barrier, inc=1, device_id={"wide": 2 * chip_there + 1, "chain": plane_there},
            device_id_type=MESH,
        )

    @pl.when(owns)
    def _():
        to_plane(GREETED, far, greet)

        def greet_later(i, _):
            greet(z_chip(i), i)
            return 0

        lax.fori_loop(z + 1, nz, greet_later, 0)

    @pl.when(core == 0)
    def _():
        pl.semaphore_wait(barrier, 1)
        pl.semaphore_signal(mate_here, inc=1, device_id=mate, device_id_type=MESH)

    @pl.when(core == 1)
    def _():
        pl.semaphore_wait(mate_here, 1)

    low = lax.broadcasted_iota(jnp.int32, (HEAD_DIM, PAIR), 1) < HEAD_DIM

    def pair_state(half, j):
        cols = pl.ds(pl.multiple_of((half * HALF + j) * PAIR, PAIR), PAIR)
        both = dot(k[:, cols], v[:, cols], ((0,), (0,)))
        return jnp.where(low, both[:HEAD_DIM], both[HEAD_DIM:])

    def half_state(half, first_load, out):
        for j in range(HALF):
            if j % 2 == 0:
                for load in loads[first_load + j // 2]:
                    load.wait()
            out[j * HEAD_DIM : (j + 1) * HEAD_DIM] = pair_state(half, j)

    half_state(1 - core, 0, given)

    swap = pltpu.make_async_remote_copy(
        src_ref=given, dst_ref=theirs, send_sem=mate_send.at[0],
        recv_sem=mate_recv.at[0], device_id=mate, device_id_type=MESH,
    )
    swap.start()
    half_state(core, 2, mine)
    extra = pltpu.make_async_remote_copy(
        src_ref=mine, dst_ref=first, send_sem=mate_send.at[1], recv_sem=mate_recv.at[1],
        device_id=mate, device_id_type=MESH,
    )

    @pl.when(core == 0)
    def _():
        extra.start()

    swap.wait_recv()
    for i in range(owners):
        rows = slice(i * ROWS, (i + 1) * ROWS)
        s_out[i] = (mine[rows] + theirs[rows]).astype(BF16)

    @pl.when((core == 1) & owns)
    def _():
        pl.semaphore_wait(barrier, 2 * (owners - 1 + z))

    @pl.when((core == 1) & jnp.logical_not(owns))
    def _():
        pl.semaphore_wait(barrier, 2 * owners)

    @pl.when(core == 1)
    def _():
        pl.semaphore_signal(all_here, inc=1, device_id=mate, device_id_type=MESH)

    @pl.when(core == 0)
    def _():
        pl.semaphore_wait(all_here, 1)

    def send_piece(there, owner_there):
        pltpu.make_async_remote_copy(
            src_ref=s_out.at[owner_there], dst_ref=s_in.at[chip], send_sem=s_send, recv_sem=s_recv,
            device_id=plane_id(there), device_id_type=MESH,
        ).start()

    to_owners(send_piece)

    @pl.when(owns)
    def _():
        s_in[chip] = s_out[owner]

        def answer_z(i, _):
            pl.semaphore_signal(z_ready.at[z], inc=1, device_id=z_id(i), device_id_type=MESH)
            return 0

        lax.fori_loop(0, z, answer_z, 0)

    upper = lax.broadcasted_iota(jnp.int32, (row_half, row_half), 0) >= lax.broadcasted_iota(
        jnp.int32, (row_half, row_half), 1
    )
    lower = lax.broadcasted_iota(
        jnp.int32, (row_half, tokens), 0
    ) + row_half >= lax.broadcasted_iota(jnp.int32, (row_half, tokens), 1)
    lanes = lax.broadcasted_iota(jnp.int32, (1, PAIR), 1)
    keep = [
        jnp.where(lanes < HEAD_DIM, 1.0, 0.0).astype(BF16),
        jnp.where(lanes >= HEAD_DIM, 1.0, 0.0).astype(BF16),
    ]

    def spread(packed):
        return jnp.concatenate([packed * keep[0], packed * keep[1]], axis=0)

    def intra_pair(p, _):
        cols = pl.ds(pl.multiple_of(p * PAIR, PAIR), PAIR)
        qp, kp, vp = q[:, cols], k[:, cols], v[:, cols]
        top = bottom = 0.0
        for h in range(2):
            kh = kp * keep[h]
            vh = vp * keep[h]
            s_top = dot(qp[:row_half], kh[:row_half], ((1,), (1,)))
            s_top = jnp.where(upper, s_top, 0.0).astype(BF16)
            s_bot = dot(qp[row_half:], kh, ((1,), (1,)))
            s_bot = jnp.where(lower, s_bot, 0.0).astype(BF16)
            top = top + dot(s_top, vh[:row_half], ((1,), (0,)))
            bottom = bottom + dot(s_bot, vh, ((1,), (0,)))
        intra[:row_half, cols] = top
        intra[row_half:, cols] = bottom
        return 0

    q_load.wait()
    lax.fori_loop(0, PAIRS, intra_pair, 0)

    @pl.when(core == 1)
    def _():
        extra.wait_recv()
        for p in range(PAIRS):
            cols = slice(p * PAIR, (p + 1) * PAIR)
            rows = slice((p % HALF) * HEAD_DIM, (p % HALF + 1) * HEAD_DIM)
            state = (first if p < HALF else theirs)[rows].astype(BF16)
            intra[:, cols] += dot(q[:, cols], spread(state), ((1,), (0,)))

    @pl.when(core == 0)
    def _():
        extra.wait_send()

    def z_start(i, _):
        pl.semaphore_wait(z_ready.at[i], 1)
        pltpu.make_async_remote_copy(
            src_ref=z_out, dst_ref=z_in.at[z], send_sem=z_send.at[i], recv_sem=z_recv.at[z],
            device_id=z_id(i), device_id_type=MESH,
        ).start()
        return 0

    def z_take(i, acc):
        pltpu.make_async_copy(z_in.at[i], z_in.at[i], z_recv.at[i]).wait()
        return acc + z_in[i]

    soon = jnp.where(z == 0, nz // 2, nz)

    def z_done(i, _):
        pltpu.make_async_copy(z_out, z_out, z_send.at[i]).wait()
        return 0

    def send_back(there):
        pltpu.make_async_remote_copy(
            src_ref=p_out.at[there], dst_ref=p_in.at[owner], send_sem=p_send, recv_sem=p_recv.at[x // 2],
            device_id=plane_id(there), device_id_type=MESH,
        ).start()

    def wait_for(buffer, count, sem):
        pltpu.make_async_copy(buffer.at[:count], buffer.at[:count], sem).wait()

    @pl.when(owns)
    def _():
        wait_for(s_in, members - 1, s_recv)
        plane = s_in[0].astype(F32)
        for i in range(1, members):
            plane = plane + s_in[i].astype(F32)
        z_out[...] = plane
        lax.fori_loop(z + 1, soon, z_start, 0)
        run = lax.fori_loop(0, z, z_take, jnp.zeros((ROWS, PAIR), F32))
        for i in range(members):
            p_out[i] = run.astype(BF16)
            if i + 1 < members:
                run = run + s_in[i].astype(F32)
        to_plane(range(CHIPS // 2), far, send_back)
        lax.fori_loop(soon, nz, z_start, 0)
        to_plane(range(CHIPS // 2, CHIPS), far, send_back)
        p_in[owner] = p_out[chip]
        wait_for(s_out, owners - 1, s_send)
        lax.fori_loop(z + 1, nz, z_done, 0)

    @pl.when(jnp.logical_not(owns))
    def _():
        wait_for(s_out, owners, s_send)

    swap.wait_send()
    mean = jnp.where(
        lax.broadcasted_iota(jnp.int32, (QUAD, QUAD), 0) // HEAD_DIM
        == lax.broadcasted_iota(jnp.int32, (QUAD, QUAD), 1) // HEAD_DIM,
        1.0 / HEAD_DIM, 0.0,
    ).astype(BF16)
    zeros = jnp.zeros((PAIR, PAIR), BF16)

    def finish(half, part, pieces):
        cols = pl.ds(pl.multiple_of((half * HALF + part * 2) * PAIR, QUAD), QUAD)
        both = pieces[pl.ds(part * share, share)].reshape(2 * HEAD_DIM, PAIR)
        one, two = spread(both[:HEAD_DIM]), spread(both[HEAD_DIM:])
        prefix = jnp.concatenate(
            [jnp.concatenate([one, zeros], axis=1), jnp.concatenate([zeros, two], axis=1)], axis=0
        )
        value = intra[:, cols] + dot(q[:, cols], prefix, ((1,), (0,)))
        square = value * value
        coarse = square.astype(BF16)
        fine = (square - coarse.astype(F32)).astype(BF16)
        var = dot(coarse, mean, ((1,), (0,))) + dot(fine, mean, ((1,), (0,)))
        o_ref[:, cols] = (value * lax.rsqrt(var + 1e-06)).astype(BF16)

    parts = [x // 2, 1 - x // 2]
    share = owners // 2

    def forward(part):
        place = pl.ds(part * share, share)
        return pltpu.make_async_remote_copy(
            src_ref=p_in.at[place], dst_ref=p_other.at[place], send_sem=f_send.at[part],
            recv_sem=f_recv.at[part], device_id=mate, device_id_type=MESH,
        )

    for step, part in enumerate(parts):

        def arrive(count):
            wait_for(p_in, count, p_recv.at[part])

        if step == 0:
            pl.when(owns)(functools.partial(arrive, share - 1))
            pl.when(jnp.logical_not(owns))(functools.partial(arrive, share))
        else:
            arrive(share)
        forward(part).start()
        finish(core, part, p_in)
    for part in parts:
        forward(part).wait_recv()
        finish(1 - core, part, p_other)
    for part in parts:
        forward(part).wait_send()

    @pl.when(owns)
    def _():
        wait_for(p_out, members - 1, p_send)


def solution(mesh):
    nx = mesh.shape["wide"] // (2 * CHIPS)
    nz = mesh.shape["chain"]
    members, owners = nx * CHIPS, nx * OWNED

    def per_device(queries, keys, values):
        tokens, width = queries.shape
        dma = pltpu.SemaphoreType.DMA
        plain = pltpu.SemaphoreType.REGULAR
        in_hbm = [pltpu.with_memory_space_constraint(t, pltpu.HBM) for t in (queries, keys, values)]
        return pl.pallas_call(
            functools.partial(attend_kernel, nx, nz),
            out_shape=jax.ShapeDtypeStruct((tokens, width), BF16),
            in_specs=[pl.BlockSpec(memory_space=pltpu.HBM)] * 3,
            out_specs=pl.BlockSpec(memory_space=pltpu.VMEM),
            scratch_shapes=[
                pltpu.VMEM((tokens, width), BF16),
                pltpu.VMEM((tokens, width), BF16),
                pltpu.VMEM((tokens, width), BF16),
                pltpu.VMEM((tokens, width), F32),
                pltpu.VMEM((STATE, PAIR), F32),
                pltpu.VMEM((STATE, PAIR), F32),
                pltpu.VMEM((STATE, PAIR), F32),
                pltpu.VMEM((STATE, PAIR), F32),
                pltpu.VMEM((owners, ROWS, PAIR), BF16),
                pltpu.VMEM((members, ROWS, PAIR), BF16),
                pltpu.VMEM((ROWS, PAIR), F32),
                pltpu.VMEM((nz, ROWS, PAIR), F32),
                pltpu.VMEM((members, ROWS, PAIR), BF16),
                pltpu.VMEM((owners, ROWS, PAIR), BF16),
                pltpu.VMEM((owners, ROWS, PAIR), BF16),
                dma((9,)),
                dma((2,)),
                dma((2,)),
                dma,
                dma,
                dma((nz,)),
                dma((nz,)),
                dma,
                dma((2,)),
                dma((2,)),
                dma((2,)),
                plain,
                plain,
                plain((nz,)),
            ],
            compiler_params=pltpu.CompilerParams(
                collective_id=0, has_side_effects=True, vmem_limit_bytes=32 << 20
            ),
        )(*in_hbm)

    placed = P(("chain", "wide"), None)
    return jax.shard_map(
        per_device, mesh=mesh, in_specs=(placed,) * 3, out_specs=placed, check_vma=False
    )
```

```python
import functools

import jax
import jax.numpy as jnp
from jax import lax
from jax.experimental import pallas as pl
from jax.experimental.pallas import tpu as pltpu
from jax.sharding import PartitionSpec as P

HEAD_DIM = 64
PAIR = 2 * HEAD_DIM
PAIRS = 8
HALF = PAIRS // 2
CHIPS = 8
OWNED = 2
GREETED = (5, 4, 6, 3, 7, 2, 1, 0)
ROWS = 64 // OWNED
STATE = HALF * HEAD_DIM
QUAD = 2 * PAIR
BF16 = jnp.bfloat16
F32 = jnp.float32
MESH = pl.DeviceIdType.MESH


def dot(a, b, contract):
    return lax.dot_general(a, b, (contract, ((), ())), preferred_element_type=F32)


def attend_kernel(
    nx, nz, q_hbm, k_hbm, v_hbm, o_ref,
    q, k, v, intra, given, mine, theirs, first, s_out, s_in, z_out, z_in, p_out, p_in, p_other,
    in_sem, swap_send, swap_recv, mate_send, mate_recv, s_send, s_recv, z_send, z_recv, p_send, p_recv, f_send, f_recv,
    mate_here, all_here, z_ready,
):
    tokens = q.shape[0]
    row_half = tokens // 2
    members = nx * CHIPS
    owners = nx * OWNED
    wide = lax.axis_index("wide")
    z = lax.axis_index("chain")
    chip = wide // 2
    core = lax.rem(wide, 2)
    mate = {"wide": 2 * chip + 1 - core}
    x, y = chip // CHIPS, lax.rem(chip, CHIPS)
    def shift(x_there, z_there):
        return jnp.where((x_there == 0) & (z_there == 0), 1, 0)

    offset = shift(x, z)
    owns = (y >= offset) & (y < offset + OWNED)
    owner = x * OWNED + y - offset
    far = sorted(range(nx), key=lambda d: -min(d, nx - d))

    def plane_id(chip):
        return {"wide": 2 * chip + core}

    def z_chip(i):
        return chip - offset + shift(x, i)

    def z_id(i):
        return {"wide": 2 * z_chip(i) + core, "chain": i}

    def to_plane(columns, across, act):
        for there in columns:
            for d in across:
                chip_there = lax.rem(x + d, nx) * CHIPS + there
                if d:
                    act(chip_there)
                else:
                    pl.when(there != y)(functools.partial(act, chip_there))

    def to_owners(act):
        for i in range(OWNED):
            for d in far:
                x_there = lax.rem(x + d, nx)
                chip_there = x_there * CHIPS + i + shift(x_there, z)
                pl.when(chip_there != chip)(
                    functools.partial(act, chip_there, x_there * OWNED + i)
                )

    loads = []
    for c in range(4):
        half = 1 - core if c < 2 else core
        cols = pl.ds(pl.multiple_of(half * (HALF * PAIR) + (c % 2) * QUAD, QUAD), QUAD)
        pair = [
            pltpu.make_async_copy(k_hbm.at[:, cols], k.at[:, cols], in_sem.at[2 * c]),
            pltpu.make_async_copy(v_hbm.at[:, cols], v.at[:, cols], in_sem.at[2 * c + 1]),
        ]
        for load in pair:
            load.start()
        loads.append(pair)
    q_load = pltpu.make_async_copy(q_hbm, q, in_sem.at[8])
    q_load.start()

    barrier = pltpu.get_barrier_semaphore()

    @pl.when(core == 1)
    def _():
        pl.semaphore_signal(barrier, inc=1, device_id=mate, device_id_type=MESH)

    def greet(chip_there, plane_there=z):
        pl.semaphore_signal(
            barrier, inc=1, device_id={"wide": 2 * chip_there + 1, "chain": plane_there},
            device_id_type=MESH,
        )

    @pl.when(owns)
    def _():
        to_plane(GREETED, far, greet)

        def greet_later(i, _):
            greet(z_chip(i), i)
            return 0

        lax.fori_loop(z + 1, nz, greet_later, 0)

    @pl.when(core == 0)
    def _():
        pl.semaphore_wait(barrier, 1)
        pl.semaphore_signal(mate_here, inc=1, device_id=mate, device_id_type=MESH)

    @pl.when(core == 1)
    def _():
        pl.semaphore_wait(mate_here, 1)

    low = lax.broadcasted_iota(jnp.int32, (HEAD_DIM, PAIR), 1) < HEAD_DIM

    def pair_state(half, j):
        cols = pl.ds(pl.multiple_of((half * HALF + j) * PAIR, PAIR), PAIR)
        both = dot(k[:, cols], v[:, cols], ((0,), (0,)))
        return jnp.where(low, both[:HEAD_DIM], both[HEAD_DIM:])

    def half_state(half, first_load, out, then=None):
        for j in range(HALF):
            if j % 2 == 0:
                for load in loads[first_load + j // 2]:
                    load.wait()
            out[j * HEAD_DIM : (j + 1) * HEAD_DIM] = pair_state(half, j)
            if j % 2 == 1 and then is not None:
                then(j // 2)

    def swap(part):
        rows = pl.ds(part * 2 * HEAD_DIM, 2 * HEAD_DIM)
        return pltpu.make_async_remote_copy(
            src_ref=given.at[rows], dst_ref=theirs.at[rows], send_sem=swap_send.at[part],
            recv_sem=swap_recv.at[part], device_id=mate, device_id_type=MESH,
        )

    half_state(1 - core, 0, given, lambda part: swap(part).start())
    half_state(core, 2, mine)
    extra = pltpu.make_async_remote_copy(
        src_ref=mine, dst_ref=first, send_sem=mate_send, recv_sem=mate_recv,
        device_id=mate, device_id_type=MESH,
    )

    @pl.when(core == 0)
    def _():
        extra.start()

    for i in range(owners):
        if i % (owners // 2) == 0:
            swap(i // (owners // 2)).wait_recv()
        rows = slice(i * ROWS, (i + 1) * ROWS)
        s_out[i] = (mine[rows] + theirs[rows]).astype(BF16)

    @pl.when((core == 1) & owns)
    def _():
        pl.semaphore_wait(barrier, 2 * (owners - 1 + z))

    @pl.when((core == 1) & jnp.logical_not(owns))
    def _():
        pl.semaphore_wait(barrier, 2 * owners)

    @pl.when(core == 1)
    def _():
        pl.semaphore_signal(all_here, inc=1, device_id=mate, device_id_type=MESH)

    @pl.when(core == 0)
    def _():
        pl.semaphore_wait(all_here, 1)

    def send_piece(there, owner_there):
        pltpu.make_async_remote_copy(
            src_ref=s_out.at[owner_there], dst_ref=s_in.at[chip], send_sem=s_send, recv_sem=s_recv,
            device_id=plane_id(there), device_id_type=MESH,
        ).start()

    to_owners(send_piece)

    @pl.when(owns)
    def _():
        s_in[chip] = s_out[owner]

        def answer_z(i, _):
            pl.semaphore_signal(z_ready.at[z], inc=1, device_id=z_id(i), device_id_type=MESH)
            return 0

        lax.fori_loop(0, z, answer_z, 0)

    upper = lax.broadcasted_iota(jnp.int32, (row_half, row_half), 0) >= lax.broadcasted_iota(
        jnp.int32, (row_half, row_half), 1
    )
    lower = lax.broadcasted_iota(
        jnp.int32, (row_half, tokens), 0
    ) + row_half >= lax.broadcasted_iota(jnp.int32, (row_half, tokens), 1)
    lanes = lax.broadcasted_iota(jnp.int32, (1, PAIR), 1)
    keep = [
        jnp.where(lanes < HEAD_DIM, 1.0, 0.0).astype(BF16),
        jnp.where(lanes >= HEAD_DIM, 1.0, 0.0).astype(BF16),
    ]

    def spread(packed):
        return jnp.concatenate([packed * keep[0], packed * keep[1]], axis=0)

    def intra_pair(p, _):
        cols = pl.ds(pl.multiple_of(p * PAIR, PAIR), PAIR)
        qp, kp, vp = q[:, cols], k[:, cols], v[:, cols]
        top = bottom = 0.0
        for h in range(2):
            kh = kp * keep[h]
            vh = vp * keep[h]
            s_top = dot(qp[:row_half], kh[:row_half], ((1,), (1,)))
            s_top = jnp.where(upper, s_top, 0.0).astype(BF16)
            s_bot = dot(qp[row_half:], kh, ((1,), (1,)))
            s_bot = jnp.where(lower, s_bot, 0.0).astype(BF16)
            top = top + dot(s_top, vh[:row_half], ((1,), (0,)))
            bottom = bottom + dot(s_bot, vh, ((1,), (0,)))
        intra[:row_half, cols] = top
        intra[row_half:, cols] = bottom
        return 0

    q_load.wait()
    lax.fori_loop(0, PAIRS, intra_pair, 0)

    @pl.when(core == 1)
    def _():
        extra.wait_recv()
        for p in range(PAIRS):
            cols = slice(p * PAIR, (p + 1) * PAIR)
            rows = slice((p % HALF) * HEAD_DIM, (p % HALF + 1) * HEAD_DIM)
            state = (first if p < HALF else theirs)[rows].astype(BF16)
            intra[:, cols] += dot(q[:, cols], spread(state), ((1,), (0,)))

    @pl.when(core == 0)
    def _():
        extra.wait_send()

    def z_start(i, _):
        pl.semaphore_wait(z_ready.at[i], 1)
        pltpu.make_async_remote_copy(
            src_ref=z_out, dst_ref=z_in.at[z], send_sem=z_send.at[i], recv_sem=z_recv.at[z],
            device_id=z_id(i), device_id_type=MESH,
        ).start()
        return 0

    def z_take(i, acc):
        pltpu.make_async_copy(z_in.at[i], z_in.at[i], z_recv.at[i]).wait()
        return acc + z_in[i]

    soon = jnp.where(z == 0, nz // 2, nz)

    def z_done(i, _):
        pltpu.make_async_copy(z_out, z_out, z_send.at[i]).wait()
        return 0

    def send_back(there):
        pltpu.make_async_remote_copy(
            src_ref=p_out.at[there], dst_ref=p_in.at[owner], send_sem=p_send, recv_sem=p_recv.at[x // 2],
            device_id=plane_id(there), device_id_type=MESH,
        ).start()

    def wait_for(buffer, count, sem):
        pltpu.make_async_copy(buffer.at[:count], buffer.at[:count], sem).wait()

    @pl.when(owns)
    def _():
        wait_for(s_in, members - 1, s_recv)
        plane = s_in[0].astype(F32)
        for i in range(1, members):
            plane = plane + s_in[i].astype(F32)
        z_out[...] = plane
        lax.fori_loop(z + 1, soon, z_start, 0)
        run = lax.fori_loop(0, z, z_take, jnp.zeros((ROWS, PAIR), F32))
        for i in range(members):
            p_out[i] = run.astype(BF16)
            if i + 1 < members:
                run = run + s_in[i].astype(F32)
        to_plane(range(CHIPS // 2), far, send_back)
        lax.fori_loop(soon, nz, z_start, 0)
        to_plane(range(CHIPS // 2, CHIPS), far, send_back)
        p_in[owner] = p_out[chip]
        wait_for(s_out, owners - 1, s_send)
        lax.fori_loop(z + 1, nz, z_done, 0)

    @pl.when(jnp.logical_not(owns))
    def _():
        wait_for(s_out, owners, s_send)

    for part in range(2):
        swap(part).wait_send()
    mean = jnp.where(
        lax.broadcasted_iota(jnp.int32, (QUAD, QUAD), 0) // HEAD_DIM
        == lax.broadcasted_iota(jnp.int32, (QUAD, QUAD), 1) // HEAD_DIM,
        1.0 / HEAD_DIM, 0.0,
    ).astype(BF16)
    zeros = jnp.zeros((PAIR, PAIR), BF16)

    def finish(half, part, pieces):
        cols = pl.ds(pl.multiple_of((half * HALF + part * 2) * PAIR, QUAD), QUAD)
        both = pieces[pl.ds(part * share, share)].reshape(2 * HEAD_DIM, PAIR)
        one, two = spread(both[:HEAD_DIM]), spread(both[HEAD_DIM:])
        prefix = jnp.concatenate(
            [jnp.concatenate([one, zeros], axis=1), jnp.concatenate([zeros, two], axis=1)], axis=0
        )
        value = intra[:, cols] + dot(q[:, cols], prefix, ((1,), (0,)))
        square = value * value
        coarse = square.astype(BF16)
        fine = (square - coarse.astype(F32)).astype(BF16)
        var = dot(coarse, mean, ((1,), (0,))) + dot(fine, mean, ((1,), (0,)))
        o_ref[:, cols] = (value * lax.rsqrt(var + 1e-06)).astype(BF16)

    parts = [x // 2, 1 - x // 2]
    share = owners // 2

    def forward(part):
        place = pl.ds(part * share, share)
        return pltpu.make_async_remote_copy(
            src_ref=p_in.at[place], dst_ref=p_other.at[place], send_sem=f_send.at[part],
            recv_sem=f_recv.at[part], device_id=mate, device_id_type=MESH,
        )

    for step, part in enumerate(parts):

        def arrive(count):
            wait_for(p_in, count, p_recv.at[part])

        if step == 0:
            pl.when(owns)(functools.partial(arrive, share - 1))
            pl.when(jnp.logical_not(owns))(functools.partial(arrive, share))
        else:
            arrive(share)
        forward(part).start()
        finish(core, part, p_in)
    for part in parts:
        forward(part).wait_recv()
        finish(1 - core, part, p_other)
    for part in parts:
        forward(part).wait_send()

    @pl.when(owns)
    def _():
        wait_for(p_out, members - 1, p_send)


def solution(mesh):
    nx = mesh.shape["wide"] // (2 * CHIPS)
    nz = mesh.shape["chain"]
    members, owners = nx * CHIPS, nx * OWNED

    def per_device(queries, keys, values):
        tokens, width = queries.shape
        dma = pltpu.SemaphoreType.DMA
        plain = pltpu.SemaphoreType.REGULAR
        in_hbm = [pltpu.with_memory_space_constraint(t, pltpu.HBM) for t in (queries, keys, values)]
        return pl.pallas_call(
            functools.partial(attend_kernel, nx, nz),
            out_shape=jax.ShapeDtypeStruct((tokens, width), BF16),
            in_specs=[pl.BlockSpec(memory_space=pltpu.HBM)] * 3,
            out_specs=pl.BlockSpec(memory_space=pltpu.VMEM),
            scratch_shapes=[
                pltpu.VMEM((tokens, width), BF16),
                pltpu.VMEM((tokens, width), BF16),
                pltpu.VMEM((tokens, width), BF16),
                pltpu.VMEM((tokens, width), F32),
                pltpu.VMEM((STATE, PAIR), F32),
                pltpu.VMEM((STATE, PAIR), F32),
                pltpu.VMEM((STATE, PAIR), F32),
                pltpu.VMEM((STATE, PAIR), F32),
                pltpu.VMEM((owners, ROWS, PAIR), BF16),
                pltpu.VMEM((members, ROWS, PAIR), BF16),
                pltpu.VMEM((ROWS, PAIR), F32),
                pltpu.VMEM((nz, ROWS, PAIR), F32),
                pltpu.VMEM((members, ROWS, PAIR), BF16),
                pltpu.VMEM((owners, ROWS, PAIR), BF16),
                pltpu.VMEM((owners, ROWS, PAIR), BF16),
                dma((9,)),
                dma((2,)),
                dma((2,)),
                dma,
                dma,
                dma,
                dma,
                dma((nz,)),
                dma((nz,)),
                dma,
                dma((2,)),
                dma((2,)),
                dma((2,)),
                plain,
                plain,
                plain((nz,)),
            ],
            compiler_params=pltpu.CompilerParams(
                collective_id=0, has_side_effects=True, vmem_limit_bytes=32 << 20
            ),
        )(*in_hbm)

    placed = P(("chain", "wide"), None)
    return jax.shard_map(
        per_device, mesh=mesh, in_specs=(placed,) * 3, out_specs=placed, check_vma=False
    )
```

```python
import functools

import jax
import jax.numpy as jnp
from jax import lax
from jax.experimental import pallas as pl
from jax.experimental.pallas import tpu as pltpu
from jax.sharding import PartitionSpec as P

HEAD_DIM = 64
PAIR = 2 * HEAD_DIM
PAIRS = 8
HALF = PAIRS // 2
CHIPS = 8
OWNED = 2
GREETED = (5, 4, 6, 3, 7, 2, 1, 0)
ROWS = 64 // OWNED
STATE = HALF * HEAD_DIM
QUAD = 2 * PAIR
BF16 = jnp.bfloat16
F32 = jnp.float32
MESH = pl.DeviceIdType.MESH


def dot(a, b, contract):
    return lax.dot_general(a, b, (contract, ((), ())), preferred_element_type=F32)


def attend_kernel(
    nx, nz, q_hbm, k_hbm, v_hbm, o_ref,
    q, k, v, intra, given, mine, theirs, first, s_out, s_in, z_out, z_in, p_out, p_in, p_other,
    in_sem, swap_send, swap_recv, mate_send, mate_recv, s_send, s_recv, z_send, z_recv, p_send, p_recv, f_send, f_recv,
    mate_here, all_here, z_ready,
):
    tokens = q.shape[0]
    row_half = tokens // 2
    members = nx * CHIPS
    owners = nx * OWNED
    wide = lax.axis_index("wide")
    z = lax.axis_index("chain")
    chip = wide // 2
    core = lax.rem(wide, 2)
    mate = {"wide": 2 * chip + 1 - core}
    x, y = chip // CHIPS, lax.rem(chip, CHIPS)
    def shift(x_there, z_there):
        return jnp.where((x_there == 0) & (z_there == 0), 1, 0)

    offset = shift(x, z)
    owns = (y >= offset) & (y < offset + OWNED)
    owner = x * OWNED + y - offset
    far = sorted(range(nx), key=lambda d: -min(d, nx - d))

    def plane_id(chip):
        return {"wide": 2 * chip + core}

    def z_chip(i):
        return chip - offset + shift(x, i)

    def z_id(i):
        return {"wide": 2 * z_chip(i) + core, "chain": i}

    def to_plane(columns, across, act):
        for there in columns:
            for d in across:
                chip_there = lax.rem(x + d, nx) * CHIPS + there
                if d:
                    act(chip_there)
                else:
                    pl.when(there != y)(functools.partial(act, chip_there))

    def to_owners(act):
        for i in range(OWNED):
            for d in far:
                x_there = lax.rem(x + d, nx)
                chip_there = x_there * CHIPS + i + shift(x_there, z)
                pl.when(chip_there != chip)(
                    functools.partial(act, chip_there, x_there * OWNED + i)
                )

    loads = []
    for c in range(4):
        half = 1 - core if c < 2 else core
        cols = pl.ds(pl.multiple_of(half * (HALF * PAIR) + (c % 2) * QUAD, QUAD), QUAD)
        pair = [
            pltpu.make_async_copy(k_hbm.at[:, cols], k.at[:, cols], in_sem.at[2 * c]),
            pltpu.make_async_copy(v_hbm.at[:, cols], v.at[:, cols], in_sem.at[2 * c + 1]),
        ]
        for load in pair:
            load.start()
        loads.append(pair)
    q_load = pltpu.make_async_copy(q_hbm, q, in_sem.at[8])
    q_load.start()

    barrier = pltpu.get_barrier_semaphore()

    @pl.when(core == 1)
    def _():
        pl.semaphore_signal(barrier, inc=1, device_id=mate, device_id_type=MESH)

    def greet(chip_there, plane_there=z):
        pl.semaphore_signal(
            barrier, inc=1, device_id={"wide": 2 * chip_there + 1, "chain": plane_there},
            device_id_type=MESH,
        )

    @pl.when(owns)
    def _():
        to_plane(GREETED, far, greet)

        def greet_later(i, _):
            greet(z_chip(i), i)
            return 0

        lax.fori_loop(z + 1, nz, greet_later, 0)

    @pl.when(core == 0)
    def _():
        pl.semaphore_wait(barrier, 1)
        pl.semaphore_signal(mate_here, inc=1, device_id=mate, device_id_type=MESH)

    @pl.when(core == 1)
    def _():
        pl.semaphore_wait(mate_here, 1)

    low = lax.broadcasted_iota(jnp.int32, (HEAD_DIM, PAIR), 1) < HEAD_DIM

    def pair_state(half, j):
        cols = pl.ds(pl.multiple_of((half * HALF + j) * PAIR, PAIR), PAIR)
        both = dot(k[:, cols], v[:, cols], ((0,), (0,)))
        return jnp.where(low, both[:HEAD_DIM], both[HEAD_DIM:])

    def half_state(half, first_load, out, then=None):
        for j in range(HALF):
            if j % 2 == 0:
                for load in loads[first_load + j // 2]:
                    load.wait()
            out[j * HEAD_DIM : (j + 1) * HEAD_DIM] = pair_state(half, j)
            if j % 2 == 1 and then is not None:
                then(j // 2)

    def swap(part):
        rows = pl.ds(part * 2 * HEAD_DIM, 2 * HEAD_DIM)
        return pltpu.make_async_remote_copy(
            src_ref=given.at[rows], dst_ref=theirs.at[rows], send_sem=swap_send.at[part],
            recv_sem=swap_recv.at[part], device_id=mate, device_id_type=MESH,
        )

    half_state(1 - core, 0, given, lambda part: swap(part).start())
    half_state(core, 2, mine)
    extra = pltpu.make_async_remote_copy(
        src_ref=mine, dst_ref=first, send_sem=mate_send, recv_sem=mate_recv,
        device_id=mate, device_id_type=MESH,
    )

    for i in range(owners):
        if i % (owners // 2) == 0:
            swap(i // (owners // 2)).wait_recv()
        rows = slice(i * ROWS, (i + 1) * ROWS)
        s_out[i] = (mine[rows] + theirs[rows]).astype(BF16)

    @pl.when((core == 1) & owns)
    def _():
        pl.semaphore_wait(barrier, 2 * (owners - 1 + z))

    @pl.when((core == 1) & jnp.logical_not(owns))
    def _():
        pl.semaphore_wait(barrier, 2 * owners)

    @pl.when(core == 1)
    def _():
        pl.semaphore_signal(all_here, inc=1, device_id=mate, device_id_type=MESH)

    @pl.when(core == 0)
    def _():
        pl.semaphore_wait(all_here, 1)

    def send_piece(there, owner_there):
        pltpu.make_async_remote_copy(
            src_ref=s_out.at[owner_there], dst_ref=s_in.at[chip], send_sem=s_send, recv_sem=s_recv,
            device_id=plane_id(there), device_id_type=MESH,
        ).start()

    to_owners(send_piece)

    @pl.when(core == 0)
    def _():
        extra.start()

    @pl.when(owns)
    def _():
        s_in[chip] = s_out[owner]

        def answer_z(i, _):
            pl.semaphore_signal(z_ready.at[z], inc=1, device_id=z_id(i), device_id_type=MESH)
            return 0

        lax.fori_loop(0, z, answer_z, 0)

    upper = lax.broadcasted_iota(jnp.int32, (row_half, row_half), 0) >= lax.broadcasted_iota(
        jnp.int32, (row_half, row_half), 1
    )
    lower = lax.broadcasted_iota(
        jnp.int32, (row_half, tokens), 0
    ) + row_half >= lax.broadcasted_iota(jnp.int32, (row_half, tokens), 1)
    lanes = lax.broadcasted_iota(jnp.int32, (1, PAIR), 1)
    keep = [
        jnp.where(lanes < HEAD_DIM, 1.0, 0.0).astype(BF16),
        jnp.where(lanes >= HEAD_DIM, 1.0, 0.0).astype(BF16),
    ]

    def spread(packed):
        return jnp.concatenate([packed * keep[0], packed * keep[1]], axis=0)

    def intra_pair(p, _):
        cols = pl.ds(pl.multiple_of(p * PAIR, PAIR), PAIR)
        qp, kp, vp = q[:, cols], k[:, cols], v[:, cols]
        top = bottom = 0.0
        for h in range(2):
            kh = kp * keep[h]
            vh = vp * keep[h]
            s_top = dot(qp[:row_half], kh[:row_half], ((1,), (1,)))
            s_top = jnp.where(upper, s_top, 0.0).astype(BF16)
            s_bot = dot(qp[row_half:], kh, ((1,), (1,)))
            s_bot = jnp.where(lower, s_bot, 0.0).astype(BF16)
            top = top + dot(s_top, vh[:row_half], ((1,), (0,)))
            bottom = bottom + dot(s_bot, vh, ((1,), (0,)))
        intra[:row_half, cols] = top
        intra[row_half:, cols] = bottom
        return 0

    q_load.wait()
    lax.fori_loop(0, PAIRS, intra_pair, 0)

    @pl.when(core == 1)
    def _():
        extra.wait_recv()
        for p in range(PAIRS):
            cols = slice(p * PAIR, (p + 1) * PAIR)
            rows = slice((p % HALF) * HEAD_DIM, (p % HALF + 1) * HEAD_DIM)
            state = (first if p < HALF else theirs)[rows].astype(BF16)
            intra[:, cols] += dot(q[:, cols], spread(state), ((1,), (0,)))

    @pl.when(core == 0)
    def _():
        extra.wait_send()

    def z_start(i, _):
        pl.semaphore_wait(z_ready.at[i], 1)
        pltpu.make_async_remote_copy(
            src_ref=z_out, dst_ref=z_in.at[z], send_sem=z_send.at[i], recv_sem=z_recv.at[z],
            device_id=z_id(i), device_id_type=MESH,
        ).start()
        return 0

    def z_take(i, acc):
        pltpu.make_async_copy(z_in.at[i], z_in.at[i], z_recv.at[i]).wait()
        return acc + z_in[i]

    soon = jnp.where(z == 0, nz // 2, nz)

    def z_done(i, _):
        pltpu.make_async_copy(z_out, z_out, z_send.at[i]).wait()
        return 0

    def send_back(there):
        pltpu.make_async_remote_copy(
            src_ref=p_out.at[there], dst_ref=p_in.at[owner], send_sem=p_send, recv_sem=p_recv.at[x // 2],
            device_id=plane_id(there), device_id_type=MESH,
        ).start()

    def wait_for(buffer, count, sem):
        pltpu.make_async_copy(buffer.at[:count], buffer.at[:count], sem).wait()

    @pl.when(owns)
    def _():
        wait_for(s_in, members - 1, s_recv)
        plane = s_in[0].astype(F32)
        for i in range(1, members):
            plane = plane + s_in[i].astype(F32)
        z_out[...] = plane
        lax.fori_loop(z + 1, soon, z_start, 0)
        run = lax.fori_loop(0, z, z_take, jnp.zeros((ROWS, PAIR), F32))
        for i in range(members):
            p_out[i] = run.astype(BF16)
            if i + 1 < members:
                run = run + s_in[i].astype(F32)
        to_plane(range(CHIPS // 2), far, send_back)
        lax.fori_loop(soon, nz, z_start, 0)
        to_plane(range(CHIPS // 2, CHIPS), far, send_back)
        p_in[owner] = p_out[chip]
        wait_for(s_out, owners - 1, s_send)
        lax.fori_loop(z + 1, nz, z_done, 0)

    @pl.when(jnp.logical_not(owns))
    def _():
        wait_for(s_out, owners, s_send)

    for part in range(2):
        swap(part).wait_send()
    mean = jnp.where(
        lax.broadcasted_iota(jnp.int32, (QUAD, QUAD), 0) // HEAD_DIM
        == lax.broadcasted_iota(jnp.int32, (QUAD, QUAD), 1) // HEAD_DIM,
        1.0 / HEAD_DIM, 0.0,
    ).astype(BF16)
    zeros = jnp.zeros((PAIR, PAIR), BF16)

    def finish(half, part, pieces):
        cols = pl.ds(pl.multiple_of((half * HALF + part * 2) * PAIR, QUAD), QUAD)
        both = pieces[pl.ds(part * share, share)].reshape(2 * HEAD_DIM, PAIR)
        one, two = spread(both[:HEAD_DIM]), spread(both[HEAD_DIM:])
        prefix = jnp.concatenate(
            [jnp.concatenate([one, zeros], axis=1), jnp.concatenate([zeros, two], axis=1)], axis=0
        )
        value = intra[:, cols] + dot(q[:, cols], prefix, ((1,), (0,)))
        square = value * value
        coarse = square.astype(BF16)
        fine = (square - coarse.astype(F32)).astype(BF16)
        var = dot(coarse, mean, ((1,), (0,))) + dot(fine, mean, ((1,), (0,)))
        o_ref[:, cols] = (value * lax.rsqrt(var + 1e-06)).astype(BF16)

    parts = [x // 2, 1 - x // 2]
    share = owners // 2

    def forward(part):
        place = pl.ds(part * share, share)
        return pltpu.make_async_remote_copy(
            src_ref=p_in.at[place], dst_ref=p_other.at[place], send_sem=f_send.at[part],
            recv_sem=f_recv.at[part], device_id=mate, device_id_type=MESH,
        )

    for step, part in enumerate(parts):

        def arrive(count):
            wait_for(p_in, count, p_recv.at[part])

        if step == 0:
            pl.when(owns)(functools.partial(arrive, share - 1))
            pl.when(jnp.logical_not(owns))(functools.partial(arrive, share))
        else:
            arrive(share)
        forward(part).start()
        finish(core, part, p_in)
    for part in parts:
        forward(part).wait_recv()
        finish(1 - core, part, p_other)
    for part in parts:
        forward(part).wait_send()

    @pl.when(owns)
    def _():
        wait_for(p_out, members - 1, p_send)


def solution(mesh):
    nx = mesh.shape["wide"] // (2 * CHIPS)
    nz = mesh.shape["chain"]
    members, owners = nx * CHIPS, nx * OWNED

    def per_device(queries, keys, values):
        tokens, width = queries.shape
        dma = pltpu.SemaphoreType.DMA
        plain = pltpu.SemaphoreType.REGULAR
        in_hbm = [pltpu.with_memory_space_constraint(t, pltpu.HBM) for t in (queries, keys, values)]
        return pl.pallas_call(
            functools.partial(attend_kernel, nx, nz),
            out_shape=jax.ShapeDtypeStruct((tokens, width), BF16),
            in_specs=[pl.BlockSpec(memory_space=pltpu.HBM)] * 3,
            out_specs=pl.BlockSpec(memory_space=pltpu.VMEM),
            scratch_shapes=[
                pltpu.VMEM((tokens, width), BF16),
                pltpu.VMEM((tokens, width), BF16),
                pltpu.VMEM((tokens, width), BF16),
                pltpu.VMEM((tokens, width), F32),
                pltpu.VMEM((STATE, PAIR), F32),
                pltpu.VMEM((STATE, PAIR), F32),
                pltpu.VMEM((STATE, PAIR), F32),
                pltpu.VMEM((STATE, PAIR), F32),
                pltpu.VMEM((owners, ROWS, PAIR), BF16),
                pltpu.VMEM((members, ROWS, PAIR), BF16),
                pltpu.VMEM((ROWS, PAIR), F32),
                pltpu.VMEM((nz, ROWS, PAIR), F32),
                pltpu.VMEM((members, ROWS, PAIR), BF16),
                pltpu.VMEM((owners, ROWS, PAIR), BF16),
                pltpu.VMEM((owners, ROWS, PAIR), BF16),
                dma((9,)),
                dma((2,)),
                dma((2,)),
                dma,
                dma,
                dma,
                dma,
                dma((nz,)),
                dma((nz,)),
                dma,
                dma((2,)),
                dma((2,)),
                dma((2,)),
                plain,
                plain,
                plain((nz,)),
            ],
            compiler_params=pltpu.CompilerParams(
                collective_id=0, has_side_effects=True, vmem_limit_bytes=32 << 20
            ),
        )(*in_hbm)

    placed = P(("chain", "wide"), None)
    return jax.shard_map(
        per_device, mesh=mesh, in_specs=(placed,) * 3, out_specs=placed, check_vma=False
    )
```

```python
import functools

import jax
import jax.numpy as jnp
from jax import lax
from jax.experimental import pallas as pl
from jax.experimental.pallas import tpu as pltpu
from jax.sharding import PartitionSpec as P

HEAD_DIM = 64
PAIR = 2 * HEAD_DIM
PAIRS = 8
HALF = PAIRS // 2
CHIPS = 8
OWNED = 2
GREETED = (5, 4, 6, 3, 7, 2, 1, 0)
ROWS = 64 // OWNED
STATE = HALF * HEAD_DIM
QUAD = 2 * PAIR
BF16 = jnp.bfloat16
F32 = jnp.float32
MESH = pl.DeviceIdType.MESH


def dot(a, b, contract):
    return lax.dot_general(a, b, (contract, ((), ())), preferred_element_type=F32)


def attend_kernel(
    nx, nz, q_hbm, k_hbm, v_hbm, o_ref,
    q, k, v, intra, given, mine, theirs, first, s_out, s_in, z_out, z_in, p_out, p_in, p_other,
    in_sem, swap_send, swap_recv, mate_send, mate_recv, s_send, s_recv, z_send, z_recv, p_send, p_recv, f_send, f_recv,
    mate_here, all_here, z_ready,
):
    tokens = q.shape[0]
    row_half = tokens // 2
    members = nx * CHIPS
    owners = nx * OWNED
    wide = lax.axis_index("wide")
    z = lax.axis_index("chain")
    chip = wide // 2
    core = lax.rem(wide, 2)
    mate = {"wide": 2 * chip + 1 - core}
    x, y = chip // CHIPS, lax.rem(chip, CHIPS)
    def shift(x_there, z_there):
        return jnp.where((x_there == 0) & (z_there == 0), 1, 0)

    offset = shift(x, z)
    owns = (y >= offset) & (y < offset + OWNED)
    owner = x * OWNED + y - offset
    far = sorted(range(nx), key=lambda d: -min(d, nx - d))

    def plane_id(chip):
        return {"wide": 2 * chip + core}

    def z_chip(i):
        return chip - offset + shift(x, i)

    def z_id(i):
        return {"wide": 2 * z_chip(i) + core, "chain": i}

    def to_plane(columns, across, act):
        for there in columns:
            for d in across:
                chip_there = lax.rem(x + d, nx) * CHIPS + there
                if d:
                    act(chip_there)
                else:
                    pl.when(there != y)(functools.partial(act, chip_there))

    def to_owners(act):
        for i in range(OWNED)[::-1]:
            for d in far:
                x_there = lax.rem(x + d, nx)
                chip_there = x_there * CHIPS + i + shift(x_there, z)
                pl.when(chip_there != chip)(
                    functools.partial(act, chip_there, x_there * OWNED + i)
                )

    loads = []
    for c in range(4):
        half = 1 - core if c < 2 else core
        cols = pl.ds(pl.multiple_of(half * (HALF * PAIR) + (c % 2) * QUAD, QUAD), QUAD)
        pair = [
            pltpu.make_async_copy(k_hbm.at[:, cols], k.at[:, cols], in_sem.at[2 * c]),
            pltpu.make_async_copy(v_hbm.at[:, cols], v.at[:, cols], in_sem.at[2 * c + 1]),
        ]
        for load in pair:
            load.start()
        loads.append(pair)
    q_load = pltpu.make_async_copy(q_hbm, q, in_sem.at[8])
    q_load.start()

    barrier = pltpu.get_barrier_semaphore()

    @pl.when(core == 1)
    def _():
        pl.semaphore_signal(barrier, inc=1, device_id=mate, device_id_type=MESH)

    def greet(chip_there, plane_there=z):
        pl.semaphore_signal(
            barrier, inc=1, device_id={"wide": 2 * chip_there + 1, "chain": plane_there},
            device_id_type=MESH,
        )

    @pl.when(owns)
    def _():
        to_plane(GREETED, far, greet)

        def greet_later(i, _):
            greet(z_chip(i), i)
            return 0

        lax.fori_loop(z + 1, nz, greet_later, 0)

    @pl.when(core == 0)
    def _():
        pl.semaphore_wait(barrier, 1)
        pl.semaphore_signal(mate_here, inc=1, device_id=mate, device_id_type=MESH)

    @pl.when(core == 1)
    def _():
        pl.semaphore_wait(mate_here, 1)

    low = lax.broadcasted_iota(jnp.int32, (HEAD_DIM, PAIR), 1) < HEAD_DIM

    def pair_state(half, j):
        cols = pl.ds(pl.multiple_of((half * HALF + j) * PAIR, PAIR), PAIR)
        both = dot(k[:, cols], v[:, cols], ((0,), (0,)))
        return jnp.where(low, both[:HEAD_DIM], both[HEAD_DIM:])

    def half_state(half, first_load, out, then=None):
        for j in range(HALF):
            if j % 2 == 0:
                for load in loads[first_load + j // 2]:
                    load.wait()
            out[j * HEAD_DIM : (j + 1) * HEAD_DIM] = pair_state(half, j)
            if j % 2 == 1 and then is not None:
                then(j // 2)

    def swap(part):
        rows = pl.ds(part * 2 * HEAD_DIM, 2 * HEAD_DIM)
        return pltpu.make_async_remote_copy(
            src_ref=given.at[rows], dst_ref=theirs.at[rows], send_sem=swap_send.at[part],
            recv_sem=swap_recv.at[part], device_id=mate, device_id_type=MESH,
        )

    half_state(1 - core, 0, given, lambda part: swap(part).start())
    half_state(core, 2, mine)
    extra = pltpu.make_async_remote_copy(
        src_ref=mine, dst_ref=first, send_sem=mate_send, recv_sem=mate_recv,
        device_id=mate, device_id_type=MESH,
    )

    for i in range(owners):
        if i % (owners // 2) == 0:
            swap(i // (owners // 2)).wait_recv()
        rows = slice(i * ROWS, (i + 1) * ROWS)
        s_out[i] = (mine[rows] + theirs[rows]).astype(BF16)

    @pl.when((core == 1) & owns)
    def _():
        pl.semaphore_wait(barrier, 2 * (owners - 1 + z))

    @pl.when((core == 1) & jnp.logical_not(owns))
    def _():
        pl.semaphore_wait(barrier, 2 * owners)

    @pl.when(core == 1)
    def _():
        pl.semaphore_signal(all_here, inc=1, device_id=mate, device_id_type=MESH)

    @pl.when(core == 0)
    def _():
        pl.semaphore_wait(all_here, 1)

    def send_piece(there, owner_there):
        pltpu.make_async_remote_copy(
            src_ref=s_out.at[owner_there], dst_ref=s_in.at[chip], send_sem=s_send, recv_sem=s_recv,
            device_id=plane_id(there), device_id_type=MESH,
        ).start()

    to_owners(send_piece)

    @pl.when(core == 0)
    def _():
        extra.start()

    @pl.when(owns)
    def _():
        s_in[chip] = s_out[owner]

        def answer_z(i, _):
            pl.semaphore_signal(z_ready.at[z], inc=1, device_id=z_id(i), device_id_type=MESH)
            return 0

        lax.fori_loop(0, z, answer_z, 0)

    upper = lax.broadcasted_iota(jnp.int32, (row_half, row_half), 0) >= lax.broadcasted_iota(
        jnp.int32, (row_half, row_half), 1
    )
    lower = lax.broadcasted_iota(
        jnp.int32, (row_half, tokens), 0
    ) + row_half >= lax.broadcasted_iota(jnp.int32, (row_half, tokens), 1)
    lanes = lax.broadcasted_iota(jnp.int32, (1, PAIR), 1)
    keep = [
        jnp.where(lanes < HEAD_DIM, 1.0, 0.0).astype(BF16),
        jnp.where(lanes >= HEAD_DIM, 1.0, 0.0).astype(BF16),
    ]

    def spread(packed):
        return jnp.concatenate([packed * keep[0], packed * keep[1]], axis=0)

    def intra_pair(p, _):
        cols = pl.ds(pl.multiple_of(p * PAIR, PAIR), PAIR)
        qp, kp, vp = q[:, cols], k[:, cols], v[:, cols]
        top = bottom = 0.0
        for h in range(2):
            kh = kp * keep[h]
            vh = vp * keep[h]
            s_top = dot(qp[:row_half], kh[:row_half], ((1,), (1,)))
            s_top = jnp.where(upper, s_top, 0.0).astype(BF16)
            s_bot = dot(qp[row_half:], kh, ((1,), (1,)))
            s_bot = jnp.where(lower, s_bot, 0.0).astype(BF16)
            top = top + dot(s_top, vh[:row_half], ((1,), (0,)))
            bottom = bottom + dot(s_bot, vh, ((1,), (0,)))
        intra[:row_half, cols] = top
        intra[row_half:, cols] = bottom
        return 0

    q_load.wait()
    lax.fori_loop(0, PAIRS, intra_pair, 0)

    @pl.when(core == 1)
    def _():
        extra.wait_recv()
        for p in range(PAIRS):
            cols = slice(p * PAIR, (p + 1) * PAIR)
            rows = slice((p % HALF) * HEAD_DIM, (p % HALF + 1) * HEAD_DIM)
            state = (first if p < HALF else theirs)[rows].astype(BF16)
            intra[:, cols] += dot(q[:, cols], spread(state), ((1,), (0,)))

    @pl.when(core == 0)
    def _():
        extra.wait_send()

    def z_start(i, _):
        pl.semaphore_wait(z_ready.at[i], 1)
        pltpu.make_async_remote_copy(
            src_ref=z_out, dst_ref=z_in.at[z], send_sem=z_send.at[i], recv_sem=z_recv.at[z],
            device_id=z_id(i), device_id_type=MESH,
        ).start()
        return 0

    def z_take(i, acc):
        pltpu.make_async_copy(z_in.at[i], z_in.at[i], z_recv.at[i]).wait()
        return acc + z_in[i]

    soon = jnp.where(z == 0, nz // 2, nz)

    def z_done(i, _):
        pltpu.make_async_copy(z_out, z_out, z_send.at[i]).wait()
        return 0

    def send_back(there):
        pltpu.make_async_remote_copy(
            src_ref=p_out.at[there], dst_ref=p_in.at[owner], send_sem=p_send, recv_sem=p_recv.at[x // 2],
            device_id=plane_id(there), device_id_type=MESH,
        ).start()

    def wait_for(buffer, count, sem):
        pltpu.make_async_copy(buffer.at[:count], buffer.at[:count], sem).wait()

    @pl.when(owns)
    def _():
        wait_for(s_in, members - 1, s_recv)
        plane = s_in[0].astype(F32)
        for i in range(1, members):
            plane = plane + s_in[i].astype(F32)
        z_out[...] = plane
        lax.fori_loop(z + 1, soon, z_start, 0)
        run = lax.fori_loop(0, z, z_take, jnp.zeros((ROWS, PAIR), F32))
        for i in range(members):
            p_out[i] = run.astype(BF16)
            if i + 1 < members:
                run = run + s_in[i].astype(F32)
        to_plane(range(CHIPS), far, send_back)
        lax.fori_loop(soon, nz, z_start, 0)
        p_in[owner] = p_out[chip]
        wait_for(s_out, owners - 1, s_send)
        lax.fori_loop(z + 1, nz, z_done, 0)

    @pl.when(jnp.logical_not(owns))
    def _():
        wait_for(s_out, owners, s_send)

    for part in range(2):
        swap(part).wait_send()
    mean = jnp.where(
        lax.broadcasted_iota(jnp.int32, (QUAD, QUAD), 0) // HEAD_DIM
        == lax.broadcasted_iota(jnp.int32, (QUAD, QUAD), 1) // HEAD_DIM,
        1.0 / HEAD_DIM, 0.0,
    ).astype(BF16)
    zeros = jnp.zeros((PAIR, PAIR), BF16)

    def finish(half, part, pieces):
        cols = pl.ds(pl.multiple_of((half * HALF + part * 2) * PAIR, QUAD), QUAD)
        both = pieces[pl.ds(part * share, share)].reshape(2 * HEAD_DIM, PAIR)
        one, two = spread(both[:HEAD_DIM]), spread(both[HEAD_DIM:])
        prefix = jnp.concatenate(
            [jnp.concatenate([one, zeros], axis=1), jnp.concatenate([zeros, two], axis=1)], axis=0
        )
        value = intra[:, cols] + dot(q[:, cols], prefix, ((1,), (0,)))
        square = value * value
        coarse = square.astype(BF16)
        fine = (square - coarse.astype(F32)).astype(BF16)
        var = dot(coarse, mean, ((1,), (0,))) + dot(fine, mean, ((1,), (0,)))
        o_ref[:, cols] = (value * lax.rsqrt(var + 1e-06)).astype(BF16)

    parts = [x // 2, 1 - x // 2]
    share = owners // 2

    def forward(part):
        place = pl.ds(part * share, share)
        return pltpu.make_async_remote_copy(
            src_ref=p_in.at[place], dst_ref=p_other.at[place], send_sem=f_send.at[part],
            recv_sem=f_recv.at[part], device_id=mate, device_id_type=MESH,
        )

    for step, part in enumerate(parts):

        def arrive(count):
            wait_for(p_in, count, p_recv.at[part])

        if step == 0:
            pl.when(owns)(functools.partial(arrive, share - 1))
            pl.when(jnp.logical_not(owns))(functools.partial(arrive, share))
        else:
            arrive(share)
        forward(part).start()
        finish(core, part, p_in)
    for part in parts:
        forward(part).wait_recv()
        finish(1 - core, part, p_other)
    for part in parts:
        forward(part).wait_send()

    @pl.when(owns)
    def _():
        wait_for(p_out, members - 1, p_send)


def solution(mesh):
    nx = mesh.shape["wide"] // (2 * CHIPS)
    nz = mesh.shape["chain"]
    members, owners = nx * CHIPS, nx * OWNED

    def per_device(queries, keys, values):
        tokens, width = queries.shape
        dma = pltpu.SemaphoreType.DMA
        plain = pltpu.SemaphoreType.REGULAR
        in_hbm = [pltpu.with_memory_space_constraint(t, pltpu.HBM) for t in (queries, keys, values)]
        return pl.pallas_call(
            functools.partial(attend_kernel, nx, nz),
            out_shape=jax.ShapeDtypeStruct((tokens, width), BF16),
            in_specs=[pl.BlockSpec(memory_space=pltpu.HBM)] * 3,
            out_specs=pl.BlockSpec(memory_space=pltpu.VMEM),
            scratch_shapes=[
                pltpu.VMEM((tokens, width), BF16),
                pltpu.VMEM((tokens, width), BF16),
                pltpu.VMEM((tokens, width), BF16),
                pltpu.VMEM((tokens, width), F32),
                pltpu.VMEM((STATE, PAIR), F32),
                pltpu.VMEM((STATE, PAIR), F32),
                pltpu.VMEM((STATE, PAIR), F32),
                pltpu.VMEM((STATE, PAIR), F32),
                pltpu.VMEM((owners, ROWS, PAIR), BF16),
                pltpu.VMEM((members, ROWS, PAIR), BF16),
                pltpu.VMEM((ROWS, PAIR), F32),
                pltpu.VMEM((nz, ROWS, PAIR), F32),
                pltpu.VMEM((members, ROWS, PAIR), BF16),
                pltpu.VMEM((owners, ROWS, PAIR), BF16),
                pltpu.VMEM((owners, ROWS, PAIR), BF16),
                dma((9,)),
                dma((2,)),
                dma((2,)),
                dma,
                dma,
                dma,
                dma,
                dma((nz,)),
                dma((nz,)),
                dma,
                dma((2,)),
                dma((2,)),
                dma((2,)),
                plain,
                plain,
                plain((nz,)),
            ],
            compiler_params=pltpu.CompilerParams(
                collective_id=0, has_side_effects=True, vmem_limit_bytes=32 << 20
            ),
        )(*in_hbm)

    placed = P(("chain", "wide"), None)
    return jax.shard_map(
        per_device, mesh=mesh, in_specs=(placed,) * 3, out_specs=placed, check_vma=False
    )
```
